128 devices in a mesh: sec: 4 (over z), ep: 32 (over x, y, core).
Axes of the slice: x: 4, y: 4, z: 4, core: 2. Of those that a mesh axis runs over, the one named last changes fastest.
Arguments:
- queries: bfloat16 [128, 4, 128, 576], P(('sec', 'ep')), may hold values from -24 to 24, as said below
- new_latent: bfloat16 [128, 4, 576], P(('sec', 'ep')), may hold values from -5 to 5
- cache_latent: bfloat16 [128, 8192, 576], P(('sec', 'ep')), may hold values from -5 to 5
- cache_len: int32 [128], P(('sec', 'ep')), may hold values from 1 to 8192, 524288 in all
- route_ids: int32 [128, 4, 8], P(('sec', 'ep')), may hold values from 0 to 31, all different within a row; in each aligned block of 4 rows (0 to 3, 4 to 7, ..., all dimensions but the last counted through in order) at most 2 rows name the same one
- route_scores: float32 [128, 4, 8], P(('sec', 'ep')), may hold values from 0.02 to 1
- residual: bfloat16 [128, 4, 7168], P(('sec', 'ep')), may hold values from -6 to 6
- norm_gain: bfloat16 [7168], replicated, may hold values from 0.099609375 to 1.8984375
- w_uv: bfloat16 [128, 512, 128], P(('sec', 'ep')), may hold values from -0.25 to 0.25
- w_out: bfloat16 [128, 128, 7168], P(('sec', 'ep')), may hold values from -0.046875 to 0.046875
- w_gate: bfloat16 [32, 7168, 1024], P('ep', None, 'sec'), may hold values from -0.0625 to 0.0625
- w_up: bfloat16 [32, 7168, 1024], P('ep', None, 'sec'), may hold values from -0.0625 to 0.0625
- w_down: bfloat16 [32, 1024, 7168], P('ep', 'sec'), may hold values from -0.1875 to 0.1875
Outputs:
- mixed: bfloat16 [128, 4, 7168], P(('sec', 'ep'))
The draws below stay inside these ranges and needn't reach their ends.
Inputs may be any that keep to these rules, and one draw needn't show every extreme that they name: `queries`: A few heads of some rows may have a query that is a multiple of that row's new latent entry. `route_ids`: each row and step names 8 different experts; over the 4 steps of one row no expert is named more than 2 times, and in some rows one expert is named exactly 2 times.
All inputs are finite; a program needn't handle non-finite values. No bound on the sum of `cache_len` on one device may be relied on, other than what follows from the above.
Results may differ from the reference program's by a relative error of at most 0.015.
Values may be sent and summed in bfloat16 or wider, within the bound.
A program may use at most 128 MiB of HBM per device.

```python
import math
import jax
import jax.numpy as jnp
import numpy as np
from jax import lax

D = 7168
LAT = 512
ROPE = 64
KV = 576
VDIM = 128
HEADS = 128
TOPK = 8
EXPERTS = 32
FF = 1024
STEPS = 4
ROWS = 128
CACHE = 8192
CAP = 2


def shared_latent(key):
    base_rows = jax.random.normal(jax.random.fold_in(key, 11), (ROWS, KV), jnp.float32)
    offsets = jax.random.normal(jax.random.fold_in(key, 12), (ROWS, KV), jnp.float32)
    return (jnp.clip(base_rows, -4.0, 4.0), jnp.clip(offsets, -4.0, 4.0))


def draw_new_latent(key, part):
    base_rows, offsets = shared_latent(key)
    factors = 0.2 * jnp.arange(STEPS, dtype=jnp.float32) / (STEPS - 1)
    return (base_rows[:, None, :] + factors[None, :, None] * offsets[:, None, :]).astype(jnp.bfloat16)


def draw_queries(key, part):
    drawn = jax.random.normal(jax.random.fold_in(key, 24), (ROWS, STEPS, HEADS, KV), jnp.float32)
    return (1.5 * jnp.clip(drawn, -6.0, 6.0)).astype(jnp.bfloat16)


def steps_of(rng, shape, shards, low, high):
    loudness = 1.0
    for position, blocks in shards:
        heights = jax.random.uniform(jax.random.fold_in(jax.random.fold_in(rng, 6), position), (blocks,), jnp.float32, low / len(shards), high / len(shards))
        loudness = loudness * jnp.repeat(jnp.exp(heights), shape[position] // blocks).reshape((-1,) + (1,) * (len(shape) - 1 - position))
    return loudness


def length_profile(count, total, bound, skew):
    portions = [(1 << 20) // math.isqrt(standing ** skew) + 1 for standing in range(2, count + 1)]
    spare, counts = total - bound - (count - 1), [1] * (count - 1)
    while spare > 0:
        movable = [i for i in range(count - 1) if counts[i] < bound]
        mass, left = sum([portions[i] for i in movable]), spare
        for i in movable:
            addition = min(bound - counts[i], max(1, left * portions[i] // mass), spare)
            counts[i] = counts[i] + addition
            spare = spare - addition
    return np.array([bound] + counts)


def ragged_sizes(rng, amount, total, bound, skew):
    if amount == 2:
        one = jax.random.randint(rng, (), max(1, total - bound), min(bound, total - 1) + 1)
        return jnp.stack([one, total - one])
    sizes = jnp.asarray(length_profile(amount, total, bound, skew), jnp.int32)
    twos = (amount - 1) // 2
    donor, taker = sizes[1:1 + 2 * twos:2], sizes[2:2 + 2 * twos:2]
    slack = jnp.minimum(donor - 1, bound - taker)
    passed = jax.random.randint(jax.random.fold_in(rng, 1), (twos,), 0, 1 << 20) % (slack + 1)
    sizes = sizes.at[1:1 + 2 * twos:2].set(donor - passed).at[2:2 + 2 * twos:2].set(taker + passed)
    return sizes[jax.random.permutation(jax.random.fold_in(rng, 2), amount)]


def routed_block(stream_key, own, number, rows, amount, top, bound, skew):
    sequence = jax.random.permutation(stream_key, amount)
    crowded, common = portions_of(amount, rows * top, bound, skew, True), portions_of(amount, rows * top, bound, skew, False)
    places = jnp.arange(amount)

    def named(sizes, rotation):
        used = int((sizes > 0).sum())
        fixed = max(1, used // 4)
        moved = fixed + (places - fixed + rotation * (used - fixed)) % max(1, amount - fixed)
        return jnp.zeros((amount,), jnp.int32).at[sequence[jnp.where(places < fixed, places, moved)]].set(jnp.asarray(sizes, jnp.int32))

    sizes = jnp.where(number % 4 == 0, named(crowded, number // 4), named(common, number - number // 4 - 1))
    mixed = jax.random.permutation(jax.random.fold_in(own, 3), amount)
    donor, taker = mixed[0:amount // 2 * 2:2], mixed[1:amount // 2 * 2:2]
    margin = jnp.minimum(sizes[donor] - 1, bound - sizes[taker]) // 2
    margin = jnp.where((donor == sequence[0]) | (taker == sequence[0]) | (sizes[taker] == 0), 0, jnp.maximum(margin, 0))
    moved = jax.random.randint(jax.random.fold_in(own, 4), (amount // 2,), 0, 1 << 20) % (margin + 1)
    sizes = sizes.at[donor].add(-moved).at[taker].add(moved)
    items = jnp.searchsorted(jnp.cumsum(sizes), jnp.arange(rows * top), side="right").astype(jnp.int32)
    grid = items.reshape(top, rows).T
    grid = grid[jax.random.permutation(jax.random.fold_in(own, 1), rows)]
    rotation = jax.random.randint(jax.random.fold_in(own, 2), (rows, 1), 0, top)
    return jnp.take_along_axis(grid, (jnp.arange(top)[None, :] + rotation) % top, axis=1)


def portions_of(amount, total, most, skew, full):
    portions = [(1 << 20) // math.isqrt(rank ** skew) + 1 for rank in range(1, amount + 1)]
    largest = most if full else min(most, max(-(-total // amount), total * portions[0] // sum(portions)))
    least = 1 if total - largest >= amount - 1 else 0
    given, rest = [largest] + [least] * (amount - 1), total - largest - least * (amount - 1)
    while rest > 0:
        candidates = [i for i in range(1, amount) if given[i] < largest] or [i for i in range(1, amount) if given[i] < most]
        pool, remaining = sum([portions[i] for i in candidates]), rest
        for i in candidates:
            more = min(most - given[i], max(1, remaining * portions[i] // pool), rest)
            given[i] = given[i] + more
            rest = rest - more
    return np.array(given)


def noise(rng, shape, deviation, bound, shards=(), kind=jnp.bfloat16):
    entries = jax.random.normal(rng, shape, jnp.float32) * deviation
    if len(shards) > 0:
        entries = steps_of(rng, shape, shards, -0.22, 0.18) * entries
    return jnp.clip(entries, min=-bound, max=bound).astype(kind)


def setup_inputs(seed: int = 0) -> dict:
    arg_keys = jax.random.split(jax.random.key(seed), 14)
    queries = draw_queries(jax.random.fold_in(arg_keys[13], 71), 0)
    new_latent = draw_new_latent(jax.random.fold_in(arg_keys[13], 71), 0)
    cache_latent = noise(arg_keys[2], (ROWS, CACHE, KV), 1.0, 5.0, ((0, 128),))
    cache_len = ragged_sizes(arg_keys[3], ROWS, ROWS * CACHE // 2, CACHE, 2).astype(jnp.int32)
    route_ids_keys = jax.random.split(jax.random.fold_in(arg_keys[4], 1), ROWS * STEPS // STEPS)
    route_ids_turns = jax.random.permutation(jax.random.fold_in(arg_keys[4], 3), ROWS * STEPS // STEPS)
    route_ids = jax.vmap(lambda own, number: routed_block(jax.random.fold_in(arg_keys[4], 2), own, number, STEPS, EXPERTS, TOPK, CAP, 2))(route_ids_keys, route_ids_turns).reshape((ROWS, STEPS, TOPK))
    route_scores = jnp.clip(jnp.exp(math.log(1.0) - 3.912023 * jax.random.uniform(arg_keys[5], (ROWS, STEPS, TOPK), jnp.float32) ** steps_of(arg_keys[5], (ROWS, STEPS, TOPK), ((0, 128),), -0.2, 0.2)), 0.02, 1.0)
    residual = noise(arg_keys[6], (ROWS, STEPS, D), 1.0, 6.0, ((0, 128),))
    norm_gain = jnp.clip(1.0 + 0.18 * jax.random.normal(arg_keys[7], (D,), jnp.float32), 0.099609375, 1.8984375).astype(jnp.bfloat16)
    w_uv = noise(arg_keys[8], (HEADS, LAT, VDIM), LAT ** -0.5, 0.25, ((0, 128),))
    w_out = noise(arg_keys[9], (HEADS, VDIM, D), (HEADS * VDIM) ** -0.5, 0.046875, ((0, 128),))
    w_gate = noise(arg_keys[10], (EXPERTS, D, FF), D ** -0.5, 0.0625, ((0, 32), (2, 4)))
    w_up = noise(arg_keys[11], (EXPERTS, D, FF), D ** -0.5, 0.0625, ((0, 32), (2, 4)))
    w_down = noise(arg_keys[12], (EXPERTS, FF, D), FF ** -0.5, 0.1875, ((0, 32), (1, 4)))
    return {"queries": queries, "new_latent": new_latent, "cache_latent": cache_latent, "cache_len": cache_len, "route_ids": route_ids, "route_scores": route_scores, "residual": residual, "norm_gain": norm_gain, "w_uv": w_uv, "w_out": w_out, "w_gate": w_gate, "w_up": w_up, "w_down": w_down}


def reference(queries, new_latent, cache_latent, cache_len, route_ids, route_scores, residual, norm_gain, w_uv, w_out, w_gate, w_up, w_down):
    score_scale = (VDIM + ROPE) ** (-0.5)
    key_count = CACHE + STEPS

    def one_row(packed):
        query_rows, new_keys, cached_rows, length = packed
        key_rows = jnp.concatenate([cached_rows, new_keys], 0).astype(jnp.float32)
        positions = jnp.arange(key_count, dtype=jnp.int32)
        step_ids = jnp.arange(STEPS, dtype=jnp.int32)
        old_ok = jnp.broadcast_to(positions[None, :] < length, (STEPS, key_count))
        new_ok = positions[None, :] - CACHE <= step_ids[:, None]
        visible = jnp.where(positions[None, :] < CACHE, old_ok, new_ok)
        scores = jnp.einsum('shk,tk->sht', query_rows.astype(jnp.float32), key_rows) * score_scale
        scores = jnp.where(visible[:, None, :], scores, -jnp.inf)
        largest = lax.optimization_barrier(jnp.max(scores, axis=-1, keepdims=True))
        weights = jnp.exp(scores - largest)
        denominator = lax.optimization_barrier(jnp.sum(weights, axis=-1, keepdims=True))
        rounded = lax.optimization_barrier(weights.astype(jnp.bfloat16)).astype(jnp.float32)
        summed = jnp.einsum('sht,tl->shl', rounded, key_rows[:, :LAT])
        return (summed / denominator).astype(jnp.bfloat16)
    latent_out = lax.map(one_row, (queries, new_latent, cache_latent, cache_len))
    head_values = jnp.einsum('rshl,hlv->rshv', latent_out.astype(jnp.float32), w_uv.astype(jnp.float32)).astype(jnp.bfloat16)
    flat_values = head_values.reshape(ROWS * STEPS, HEADS * VDIM)
    attended = jnp.dot(flat_values, w_out.reshape(HEADS * VDIM, D), preferred_element_type=jnp.float32)
    hidden = residual.reshape(ROWS * STEPS, D).astype(jnp.float32) + attended
    mean_square = lax.optimization_barrier(jnp.mean(hidden * hidden, axis=-1, keepdims=True))
    normed = (hidden * lax.rsqrt(mean_square + 1e-06) * norm_gain.astype(jnp.float32)).astype(jnp.bfloat16)
    shares = route_scores / lax.optimization_barrier(jnp.sum(route_scores, axis=-1, keepdims=True)) * 2.5
    matches = route_ids[..., None] == jnp.arange(EXPERTS, dtype=jnp.int32)
    coefficient = lax.optimization_barrier(jnp.sum(jnp.where(matches, shares[..., None], 0.0), axis=2)).reshape(ROWS * STEPS, EXPERTS)

    def expert_step(summed, packed):
        gate_matrix, up_matrix, down_matrix, column = packed
        gate_value = jnp.dot(normed, gate_matrix, preferred_element_type=jnp.float32)
        up_value = jnp.dot(normed, up_matrix, preferred_element_type=jnp.float32)
        activated = (jax.nn.silu(gate_value) * up_value).astype(jnp.bfloat16)
        expert_out = jnp.dot(activated, down_matrix, preferred_element_type=jnp.float32).astype(jnp.bfloat16)
        expert_out = lax.optimization_barrier(expert_out).astype(jnp.float32)
        return (summed + column[:, None] * expert_out, None)
    start_sum = jnp.zeros((ROWS * STEPS, D), jnp.float32)
    summed, _ = lax.scan(expert_step, start_sum, (w_gate, w_up, w_down, coefficient.T))
    return (hidden + summed).astype(jnp.bfloat16).reshape(ROWS, STEPS, D)
```

```python
import functools
import jax, jax.numpy as jnp
from jax import lax
from jax.experimental import pallas as pl
from jax.experimental.pallas import tpu as pltpu
from jax.sharding import PartitionSpec as P
MESH = pl.DeviceIdType.MESH
COLS = 3584
PARTS = ((0, 1280, 640, (0, 1, 2)), (1280, 1152, 640, (1, 2, 0)), (2432, 1152, 640, (2, 0, 1)))


def place():
    z = lax.axis_index("sec")
    e = lax.axis_index("ep")
    x = e // 8
    y = (e // 2) % 4
    c = e % 2
    return (z, x, y), c


def dev(pos, c):
    return (pos[0], (pos[1] * 4 + pos[2]) * 2 + c)


def shifted(pos, axis, by):
    out = list(pos)
    out[axis] = (pos[axis] + by) % 4
    return tuple(out)


def greet_neighbours(pos, c):
    barrier = pltpu.get_barrier_semaphore()
    for axis in range(3):
        for by in (1, 3):
            pl.semaphore_signal(barrier, inc=1, device_id=dev(shifted(pos, axis, by), c), device_id_type=MESH)
    pl.semaphore_wait(barrier, 6)


def remote(src, dst, ss, rs, to):
    return pltpu.make_async_remote_copy(src_ref=src, dst_ref=dst, send_sem=ss, recv_sem=rs, device_id=to, device_id_type=MESH)


def rs_body(pos, c, acc, bufs, ss, rs):
    def region(p, stage, q, lo, hi):
        start, width, half, order = PARTS[p]
        idx = [slice(None)] * 3
        for k in range(stage):
            idx[order[k]] = pos[order[k]]
        idx[order[stage]] = q
        return tuple(idx) + (slice(None), slice(start + lo, start + hi))

    def bslot(p, stage, d, lo, hi):
        start = PARTS[p][0]
        lead = (slice(None),) * (2 - stage)
        return bufs[stage].at[(d,) + lead + (slice(None), slice(start + lo, start + hi))]

    def add(p, stage, q, d, lo, hi):
        dst = acc.at[region(p, stage, q, lo, hi)]
        src = bslot(p, stage, d, lo, hi)
        dst[...] = (dst[...].astype(jnp.float32) + src[...].astype(jnp.float32)).astype(acc.dtype)

    for stage in range(3):
        first = []
        for p in range(3):
            start, width, half, order = PARTS[p]
            axis = order[stage]
            far = (pos[axis] + 2) % 4
            for d, by, lo, hi in ((0, 1, 0, half), (1, 3, half, width)):
                cp = remote(acc.at[region(p, stage, far, lo, hi)], bslot(p, stage, 2 + d, lo, hi),
                            ss.at[p, stage, 0, d], rs.at[p, stage, 0, d], dev(shifted(pos, axis, by), c))
                cp.start()
                first.append(cp)
        second = []
        for p in range(3):
            start, width, half, order = PARTS[p]
            axis = order[stage]
            for d, by, lo, hi in ((0, 1, 0, half), (1, 3, half, width)):
                q = (pos[axis] + by) % 4
                first[p * 2 + d].wait_recv()
                add(p, stage, q, 2 + d, lo, hi)
            for d, by in ((0, 1), (1, 3)):
                q = (pos[axis] + by) % 4
                cp = remote(acc.at[region(p, stage, q, 0, width)], bslot(p, stage, d, 0, width),
                            ss.at[p, stage, 1, d], rs.at[p, stage, 1, d], dev(shifted(pos, axis, by), c))
                cp.start()
                second.append(cp)
        for p in range(3):
            start, width, half, order = PARTS[p]
            axis = order[stage]
            mine = acc.at[region(p, stage, pos[axis], 0, width)]
            second[p * 2].wait_recv()
            second[p * 2 + 1].wait_recv()
            mine[...] = (mine[...].astype(jnp.float32) + bslot(p, stage, 0, 0, width)[...].astype(jnp.float32)
                         + bslot(p, stage, 1, 0, width)[...].astype(jnp.float32)).astype(acc.dtype)
        for cp in first + second:
            cp.wait_send()


def ag_body(pos, c, g, ss, rs):
    def region(p, stage, q, lo, hi):
        start, width, half, order = PARTS[p]
        idx = [slice(None)] * 3
        for k in range(stage):
            idx[order[k]] = pos[order[k]]
        idx[order[stage]] = q
        return tuple(idx) + (slice(None), slice(start + lo, start + hi))
    sent = []
    for stage in (2, 1, 0):
        first = []
        for p in range(3):
            start, width, half, order = PARTS[p]
            axis = order[stage]
            for d, by in ((0, 1), (1, 3)):
                r = g.at[region(p, stage, pos[axis], 0, width)]
                cp = remote(r, r, ss.at[p, stage, 0, d], rs.at[p, stage, 0, d], dev(shifted(pos, axis, by), c))
                cp.start()
                first.append(cp)
        second = []
        for p in range(3):
            start, width, half, order = PARTS[p]
            axis = order[stage]
            for d, by, lo, hi in ((0, 1, 0, half), (1, 3, half, width)):
                q = (pos[axis] + 4 - by) % 4
                first[p * 2 + d].wait_recv()
                r = g.at[region(p, stage, q, lo, hi)]
                cp = remote(r, r, ss.at[p, stage, 1, d], rs.at[p, stage, 1, d], dev(shifted(pos, axis, by), c))
                cp.start()
                second.append(cp)
        for cp in second:
            cp.wait_recv()
        sent += first + second
    for cp in sent:
        cp.wait_send()


def rs_kernel(y_ref, o_ref, acc, b0, b1, b2, ss, rs, lsem):
    pos, c = place()
    cp = pltpu.make_async_copy(y_ref, acc, lsem)
    cp.start()
    greet_neighbours(pos, c)
    cp.wait()
    rs_body(pos, c, acc, (b0, b1, b2), ss, rs)
    o_ref[...] = acc[pos[0], pos[1], pos[2]].astype(jnp.float32)


def rs_call(y, cid=1):
    bf = jnp.bfloat16
    return pl.pallas_call(
        rs_kernel, out_shape=jax.ShapeDtypeStruct((8, COLS), jnp.float32),
        in_specs=[pl.BlockSpec(memory_space=pl.ANY)], out_specs=pl.BlockSpec(memory_space=pltpu.VMEM),
        scratch_shapes=[pltpu.VMEM((4, 4, 4, 8, COLS), bf), pltpu.VMEM((4, 4, 4, 8, COLS), bf), pltpu.VMEM((4, 4, 8, COLS), bf),
                        pltpu.VMEM((4, 8, COLS), bf), pltpu.SemaphoreType.DMA((3, 3, 2, 2)), pltpu.SemaphoreType.DMA((3, 3, 2, 2)), pltpu.SemaphoreType.DMA],
        compiler_params=pltpu.CompilerParams(collective_id=cid, has_side_effects=True, vmem_limit_bytes=40 << 20),
    )(y)


def ag_kernel(b_ref, o_ref, ss, rs, lsem):
    pos, c = place()
    cp = pltpu.make_async_copy(b_ref, o_ref.at[pos[0], pos[1], pos[2]], lsem)
    cp.start()
    greet_neighbours(pos, c)
    cp.wait()
    ag_body(pos, c, o_ref, ss, rs)


def ag_call(b, cid=2):
    return pl.pallas_call(
        ag_kernel, out_shape=jax.ShapeDtypeStruct((4, 4, 4, 8, COLS), jnp.bfloat16),
        in_specs=[pl.BlockSpec(memory_space=pl.ANY)], out_specs=pl.BlockSpec(memory_space=pltpu.VMEM),
        scratch_shapes=[pltpu.SemaphoreType.DMA((3, 3, 2, 2)), pltpu.SemaphoreType.DMA((3, 3, 2, 2)), pltpu.SemaphoreType.DMA],
        compiler_params=pltpu.CompilerParams(collective_id=cid, has_side_effects=True, vmem_limit_bytes=40 << 20),
    )(b)


def a2a_kernel(o_ref, x_ref, ss, rs, lsem):
    (z, x, y), c = place()
    me = z * 16 + x * 4 + y

    def peer(i):
        k = (me + i) % 64
        return k, (k // 16, (k % 16) * 2 + c)
    local = pltpu.make_async_copy(o_ref.at[me], x_ref.at[me], lsem)
    local.start()
    barrier = pltpu.get_barrier_semaphore()

    @pl.loop(1, 64)
    def _(i):
        pl.semaphore_signal(barrier, inc=1, device_id=peer(i)[1], device_id_type=MESH)
    pl.semaphore_wait(barrier, 63)

    @pl.loop(1, 64)
    def _(i):
        k, to = peer(i)
        remote(o_ref.at[k], x_ref.at[me], ss.at[i], rs.at[me], to).start()

    @pl.loop(1, 64)
    def _(i):
        k, to = peer(i)
        remote(o_ref.at[k], x_ref.at[k], ss.at[i], rs.at[k], to).wait_recv()

    @pl.loop(1, 64)
    def _(i):
        k, to = peer(i)
        remote(o_ref.at[k], x_ref.at[k], ss.at[i], rs.at[k], to).wait_send()
    local.wait()


def a2a_call(o, cid=3):
    return pl.pallas_call(
        a2a_kernel, out_shape=jax.ShapeDtypeStruct((64, 8, 512), jnp.bfloat16),
        in_specs=[pl.BlockSpec(memory_space=pltpu.VMEM)], out_specs=pl.BlockSpec(memory_space=pltpu.VMEM),
        scratch_shapes=[pltpu.SemaphoreType.DMA((64,)), pltpu.SemaphoreType.DMA((64,)), pltpu.SemaphoreType.DMA],
        compiler_params=pltpu.CompilerParams(collective_id=cid, has_side_effects=True, vmem_limit_bytes=40 << 20),
    )(o)

LAT=512; KV=576; HEADS=128; STEPS=4; CACHE=8192
LOG2E=1.4426950408889634
SCALE=(192.0)**-0.5
f32=jnp.float32; bf=jnp.bfloat16

def attn_kernel(T, RB, len_ref, qt_ref, new_ref, kt_ref, o_ref, q_sc, kbuf, m_sc, l_sc, acc_sc, sem):
    n = len_ref[0]
    nblk = (n + T - 1) // T
    ROWS = STEPS*HEADS
    c = SCALE*LOG2E

    def fetch(i, slot):
        return pltpu.make_async_copy(kt_ref.at[:, pl.ds(pl.multiple_of(i*T, T), T)], kbuf.at[slot], sem.at[slot])
    fetch(0, 0).start()
    for s in range(STEPS):
        q_sc[s*HEADS:(s+1)*HEADS, :] = qt_ref[s].T
    for s in range(STEPS):
        q = q_sc[s*HEADS:(s+1)*HEADS, :]
        sc = lax.dot_general(q, new_ref[...], (((1,),(1,)),((),())), preferred_element_type=f32) * c
        col = lax.broadcasted_iota(jnp.int32, sc.shape, 1)
        sc = jnp.where(col <= s, sc, -1e30)
        m = jnp.max(sc, axis=1, keepdims=True)
        p = jnp.exp2(sc - m)
        l = jnp.sum(p, axis=1, keepdims=True)
        m_sc[s*HEADS:(s+1)*HEADS, :] = jnp.broadcast_to(m, (HEADS, 128))
        l_sc[s*HEADS:(s+1)*HEADS, :] = jnp.broadcast_to(l, (HEADS, 128))
        acc_sc[s*HEADS:(s+1)*HEADS, :] = jnp.dot(p.astype(bf), new_ref[:, :LAT], preferred_element_type=f32)

    def block(i, masked):
        slot = lax.rem(i, 2)
        fetch(i, slot).wait()
        @pl.when(i + 1 < nblk)
        def _():
            fetch(i + 1, 1 - slot).start()
        kt = kbuf.at[slot]
        for r in range(0, ROWS, RB):
            s_ = jnp.dot(q_sc[r:r+RB, :], kt[...], preferred_element_type=f32)
            if masked:
                col = lax.broadcasted_iota(jnp.int32, (1, T), 1) + i*T
                s_ = jnp.where(col < n, s_, -1e30)
            mo = m_sc[r:r+RB, :1]
            mn = jnp.maximum(mo, jnp.max(s_, axis=1, keepdims=True) * c)
            a = jnp.exp2(mo - mn)
            p = jnp.exp2(s_ * c - mn)
            l_sc[r:r+RB, :] = l_sc[r:r+RB, :] * a + jnp.sum(p, axis=1, keepdims=True)
            pv = lax.dot_general(p.astype(bf), kt[:LAT, :], (((1,),(1,)),((),())), preferred_element_type=f32)
            acc_sc[r:r+RB, :] = acc_sc[r:r+RB, :] * a + pv
            m_sc[r:r+RB, :] = jnp.broadcast_to(mn, (RB, 128))
    nfull = n // T
    @pl.loop(0, nfull)
    def _(i):
        block(i, False)
    @pl.when(nfull < nblk)
    def _():
        block(nfull, True)
    ob = (acc_sc[...] * (1.0 / l_sc[:, :1])).astype(bf)
    i0 = lax.broadcasted_iota(jnp.int32, (ROWS, ROWS), 0)
    i1 = lax.broadcasted_iota(jnp.int32, (ROWS, ROWS), 1)
    perm = jnp.where((i0 % 4) * HEADS + i0 // 4 == i1, 1.0, 0.0).astype(bf)
    o_ref[...] = jnp.dot(perm, ob, preferred_element_type=f32).astype(bf)

def attend(queries, new_latent, cache_latent, cache_len, T=1024, RB=256):
    qt = jnp.swapaxes(queries[0], 1, 2)
    kt = jnp.swapaxes(cache_latent[0], 0, 1)
    new = jnp.pad(new_latent[0], ((0, 128 - STEPS), (0, 0)))
    return pl.pallas_call(
        functools.partial(attn_kernel, T, RB),
        out_shape=jax.ShapeDtypeStruct((STEPS*HEADS, LAT), bf),
        in_specs=[pl.BlockSpec(memory_space=pltpu.SMEM), pl.BlockSpec(memory_space=pltpu.VMEM), pl.BlockSpec(memory_space=pltpu.VMEM), pl.BlockSpec(memory_space=pl.ANY)],
        out_specs=pl.BlockSpec(memory_space=pltpu.VMEM),
        scratch_shapes=[pltpu.VMEM((STEPS*HEADS, KV), bf), pltpu.VMEM((2, KV, T), bf), pltpu.VMEM((STEPS*HEADS, 128), f32), pltpu.VMEM((STEPS*HEADS, 128), f32),
                        pltpu.VMEM((STEPS*HEADS, LAT), f32), pltpu.SemaphoreType.DMA((2,))],
        compiler_params=pltpu.CompilerParams(vmem_limit_bytes=48 << 20),
    )(cache_len, qt, new, kt)


def chip_swap(v):
    return lax.ppermute(v, "ep", [(i, i ^ 1) for i in range(32)])


def half_of(w, which, axis):
    size = w.shape[axis] // 2
    return lax.dynamic_slice_in_dim(w, which * size, size, axis)


def pair(c, mine, other, axis):
    return jnp.where(c == 0, jnp.concatenate([mine, other], axis), jnp.concatenate([other, mine], axis))


def per_device(queries, new_latent, cache_latent, cache_len, route_ids, route_scores, residual, norm_gain,
               w_uv, w_out, w_gate, w_up, w_down):
    c = lax.axis_index("ep") % 2
    mine_half = lambda w, axis: half_of(w, c, axis)
    other_half = lambda w, axis: half_of(w, 1 - c, axis)
    uv = pair(c, w_uv, chip_swap(w_uv), 0)
    wo = pair(c, mine_half(w_out[0], 1), chip_swap(other_half(w_out[0], 1)), 0)
    wg = pair(c, mine_half(w_gate[0], 0), chip_swap(other_half(w_gate[0], 0)), 1)
    wu = pair(c, mine_half(w_up[0], 0), chip_swap(other_half(w_up[0], 0)), 1)
    wd = pair(c, mine_half(w_down[0], 1), chip_swap(other_half(w_down[0], 1)), 0)
    e = lax.axis_index("ep")
    shares = route_scores[0] / jnp.sum(route_scores[0], axis=1, keepdims=True) * 2.5
    matches = route_ids[0][:, :, None] == jnp.arange(32, dtype=jnp.int32)[None, None, :]
    coefficient = jnp.sum(jnp.where(matches, shares[:, :, None], 0.0), axis=1)
    coef_all = lax.all_gather(coefficient, ("sec", "ep"), axis=0, tiled=True)
    column = lax.dynamic_slice_in_dim(coef_all, e, 1, 1)

    latent = attend(queries, new_latent, cache_latent, cache_len)
    x = a2a_call(latent.reshape(64, 8, 512))
    both = pair(c, x[None], chip_swap(x)[None], 0)
    both = both.reshape(2, 64, 2, 4, 512)
    hv = jnp.einsum("ckjsl,jlv->kcsjv", both, uv, preferred_element_type=jnp.float32).astype(jnp.bfloat16)
    y = jnp.dot(hv.reshape(512, 256), wo, preferred_element_type=jnp.float32).astype(jnp.bfloat16)
    part = rs_call(y.reshape(4, 4, 4, 8, COLS), 1)
    own = lax.dynamic_slice_in_dim(part, c * 4, 4, 0)
    other = chip_swap(lax.dynamic_slice_in_dim(part, (1 - c) * 4, 4, 0))
    hidden = residual[0].astype(jnp.float32) + pair(c, own, other, 1)
    mean_square = jnp.mean(hidden * hidden, axis=-1, keepdims=True)
    normed = (hidden * lax.rsqrt(mean_square + 1e-06) * norm_gain.astype(jnp.float32)).astype(jnp.bfloat16)
    block = pair(c, mine_half(normed, 1), chip_swap(other_half(normed, 1)), 0)
    tokens = ag_call(block, 2).reshape(512, COLS)
    gate_up = jnp.dot(tokens, jnp.concatenate([wg, wu], 1), preferred_element_type=jnp.float32)
    gu = gate_up.reshape(512, 2, 2, 256)
    gu_mine = lax.dynamic_index_in_dim(gu, c, 2, keepdims=False)
    gu_other = chip_swap(lax.dynamic_index_in_dim(gu, 1 - c, 2, keepdims=False).astype(jnp.bfloat16)).astype(jnp.float32)
    total = gu_mine + gu_other
    act = (jax.nn.silu(total[:, 0]) * total[:, 1] * column).astype(jnp.bfloat16)
    acts = pair(c, act, chip_swap(act), 1)
    y2 = jnp.dot(acts, wd, preferred_element_type=jnp.float32).astype(jnp.bfloat16)
    part2 = rs_call(y2.reshape(4, 4, 4, 8, COLS), 1)
    own2 = lax.dynamic_slice_in_dim(part2, c * 4, 4, 0)
    other2 = chip_swap(lax.dynamic_slice_in_dim(part2, (1 - c) * 4, 4, 0))
    return (hidden + pair(c, own2, other2, 1)).astype(jnp.bfloat16)[None]


def solution(mesh):
    r = ("sec", "ep")
    placed = (P(r, None, None, None), P(r, None, None), P(r, None, None), P(r), P(r, None, None), P(r, None, None), P(r, None, None),
              P(), P(r, None, None), P(r, None, None), P("ep", None, "sec"), P("ep", None, "sec"), P("ep", "sec", None))
    return jax.shard_map(per_device, mesh=mesh, in_specs=placed, out_specs=P(r, None, None), check_vma=False)
```

```python
import functools
import jax, jax.numpy as jnp
from jax import lax
from jax.experimental import pallas as pl
from jax.experimental.pallas import tpu as pltpu
from jax.sharding import PartitionSpec as P

MESH = pl.DeviceIdType.MESH
f32 = jnp.float32
bf = jnp.bfloat16
COLS = 3584
GCOLS = 3712
PARTS_RS = ((0, 1280, 640, (0, 1, 2)), (1280, 1152, 640, (1, 2, 0)), (2432, 1152, 640, (2, 0, 1)))
PARTS_AG = ((0, 1280, 640, (0, 1, 2)), (1280, 1280, 640, (1, 2, 0)), (2560, 1152, 640, (2, 0, 1)))


def dev(pos, c):
    return (pos[0], (pos[1] * 4 + pos[2]) * 2 + c)


def shifted(pos, axis, by):
    out = list(pos)
    out[axis] = (pos[axis] + by) % 4
    return tuple(out)


def remote(src, dst, ss, rs, to):
    return pltpu.make_async_remote_copy(src_ref=src, dst_ref=dst, send_sem=ss, recv_sem=rs, device_id=to, device_id_type=MESH)


def region(parts, pos, p, stage, q, lo, hi):
    start, _, _, order = parts[p]
    idx = [slice(None)] * 3
    for k in range(stage):
        idx[order[k]] = pos[order[k]]
    idx[order[stage]] = q
    return tuple(idx) + (slice(None), slice(start + lo, start + hi))


def reduce_scatter(pos, c, acc, bufs, ss, rs, out):
    def slot(p, stage, d, lo, hi):
        start = PARTS_RS[p][0]
        return bufs[stage].at[(d,) + (slice(None),) * (2 - stage) + (slice(None), slice(start + lo, start + hi))]

    def reg(p, stage, q, lo, hi):
        return acc.at[region(PARTS_RS, pos, p, stage, q, lo, hi)]

    first, second = [], []
    for p in range(3):
        _, width, half, order = PARTS_RS[p]
        axis = order[0]
        for d, by, lo, hi in ((0, 1, 0, half), (1, 3, half, width)):
            cp = remote(reg(p, 0, (pos[axis] + 2) % 4, lo, hi), slot(p, 0, 2 + d, lo, hi), ss.at[p, d], rs.at[p, d], dev(shifted(pos, axis, by), c))
            cp.start()
            first.append(cp)
    for p in range(3):
        _, width, half, order = PARTS_RS[p]
        axis = order[0]
        for d, by, lo, hi in ((0, 1, 0, half), (1, 3, half, width)):
            q = (pos[axis] + by) % 4
            first[p * 2 + d].wait_recv()
            dst = reg(p, 0, q, lo, hi)
            dst[...] = (dst[...].astype(f32) + slot(p, 0, 2 + d, lo, hi)[...].astype(f32)).astype(bf)
        for d, by in ((0, 1), (1, 3)):
            q = (pos[axis] + by) % 4
            cp = remote(reg(p, 0, q, 0, width), slot(p, 0, d, 0, width), ss.at[p, 2 + d], rs.at[p, 2 + d], dev(shifted(pos, axis, by), c))
            cp.start()
            second.append(cp)
    third = [[], []]
    for stage in (1, 2):
        for p in range(3):
            start, width, _, order = PARTS_RS[p]
            before = order[stage - 1]
            mine = reg(p, stage - 1, pos[before], 0, width)
            arrived = second[2 * p:2 * p + 2] if stage == 1 else third[0][3 * p:3 * p + 3]
            total = mine[...].astype(f32)
            for d, cp in enumerate(arrived):
                cp.wait_recv()
                total += slot(p, stage - 1, d, 0, width)[...].astype(f32)
            mine[...] = total.astype(bf)
            axis = order[stage]
            for by in (1, 2, 3):
                q = (pos[axis] + by) % 4
                n = 4 + (stage - 1) * 3 + by - 1
                cp = remote(reg(p, stage, q, 0, width), slot(p, stage, by - 1, 0, width), ss.at[p, n], rs.at[p, n], dev(shifted(pos, axis, by), c))
                cp.start()
                third[stage - 1].append(cp)
    for p in range(3):
        start, width, _, order = PARTS_RS[p]
        total = reg(p, 2, pos[order[2]], 0, width)[...].astype(f32)
        for d, cp in enumerate(third[1][3 * p:3 * p + 3]):
            cp.wait_recv()
            total += slot(p, 2, d, 0, width)[...].astype(f32)
        out[:, start:start + width] = total
    for cp in first + second + third[0] + third[1]:
        cp.wait_send()


def all_gather(pos, c, g, ss, rs):
    def reg(p, stage, q, lo, hi):
        return g.at[region(PARTS_AG, pos, p, stage, q, lo, hi)]

    sent = []
    waiting = [[], [], []]
    for stage in (2, 1):
        for p in range(3):
            _, width, _, order = PARTS_AG[p]
            axis = order[stage]
            for cp in waiting[p]:
                cp.wait_recv()
            waiting[p] = []
            for by in (1, 2, 3):
                r = reg(p, stage, pos[axis], 0, width)
                n = 4 + (stage - 1) * 3 + by - 1
                cp = remote(r, r, ss.at[p, n], rs.at[p, n], dev(shifted(pos, axis, by), c))
                cp.start()
                waiting[p].append(cp)
                sent.append(cp)
    first = []
    for p in range(3):
        _, width, half, order = PARTS_AG[p]
        axis = order[0]
        for cp in waiting[p]:
            cp.wait_recv()
        for d, by in ((0, 1), (1, 3)):
            r = reg(p, 0, pos[axis], 0, width)
            cp = remote(r, r, ss.at[p, d], rs.at[p, d], dev(shifted(pos, axis, by), c))
            cp.start()
            first.append(cp)
    second = []
    for p in range(3):
        _, width, half, order = PARTS_AG[p]
        axis = order[0]
        for d, by, lo, hi in ((0, 1, 0, half), (1, 3, half, width)):
            first[p * 2 + d].wait_recv()
            r = reg(p, 0, (pos[axis] + 4 - by) % 4, lo, hi)
            cp = remote(r, r, ss.at[p, 2 + d], rs.at[p, 2 + d], dev(shifted(pos, axis, by), c))
            cp.start()
            second.append(cp)
    for cp in second:
        cp.wait_recv()
    for cp in sent + first + second:
        cp.wait_send()


def layer_kernel(o_ref, ids_ref, sc_ref, res_ref, gain_ref, uv_hbm, wo_hbm, wg_hbm, wu_hbm, wd_hbm, out_ref,
                 x_v, uv_v, wo_v, w_v, wd_v, h_v, hs_v, acc, b0, b1, b2, part, res_v, cf_v, g_v, snd_v, rcv_v, act_v, fin_v,
                 a_ss, a_rs, l_sem, w_ss, w_rs, s_ss, s_rs, r1_ss, r1_rs, g_ss, g_rs, r2_ss, r2_rs):
    z = lax.axis_index("sec")
    e = lax.axis_index("ep")
    x, y, c = e // 8, (e // 2) % 4, e % 2
    pos = (z, x, y)
    me = z * 16 + x * 4 + y
    sib = dev(pos, 1 - c)
    mine = pl.multiple_of(c * COLS, 128)
    other = pl.multiple_of((1 - c) * COLS, 128)

    def peer(i):
        k = (me + i) % 64
        return k, (k // 16, (k % 16) * 2 + c)

    barrier = pltpu.get_barrier_semaphore()

    @pl.loop(1, 64)
    def _(i):
        pl.semaphore_signal(barrier, inc=1, device_id=peer(i)[1], device_id_type=MESH)
    pl.semaphore_signal(barrier, inc=1, device_id=sib, device_id_type=MESH)

    uvc = pl.ds(pl.multiple_of(c * 128, 128), 128)
    local = [pltpu.make_async_copy(a, b, l_sem.at[i]) for i, (a, b) in enumerate((
        (o_ref.at[me], x_v.at[me]),
        (uv_hbm, uv_v.at[:, uvc]),
        (wo_hbm.at[:, pl.ds(mine, COLS)], wo_v.at[pl.ds(pl.multiple_of(c * 128, 128), 128), :]),
        (wg_hbm.at[pl.ds(mine, COLS), :], w_v.at[c, 0]),
        (wu_hbm.at[pl.ds(mine, COLS), :], w_v.at[c, 1]),
        (wd_hbm.at[:, pl.ds(mine, COLS)], wd_v.at[c]),
        (res_ref, res_v.at[c]),
    ))]
    for cp in local[:3]:
        cp.start()
    local[6].start()
    sc = sc_ref[...]
    shares = sc / jnp.sum(sc, axis=1, keepdims=True) * 2.5
    ids = ids_ref[...]
    lane = lax.broadcasted_iota(jnp.int32, (4, 128), 1)
    coef = jnp.zeros((4, 128), f32)
    for k in range(8):
        coef += jnp.where(lane % 32 == ids[:, k:k + 1], shares[:, k:k + 1], 0.0)
    high = coef.astype(bf).astype(f32)
    cf_v[c] = jnp.where(lane < 32, high, jnp.where(lane < 64, coef - high, 0.0))

    pl.semaphore_wait(barrier, 64)

    @pl.loop(1, 64)
    def _(i):
        k, to = peer(i)
        remote(o_ref.at[k], x_v.at[me], a_ss.at[i], a_rs.at[me], to).start()

    early = [remote(a, b, w_ss.at[i], w_rs.at[i], sib) for i, (a, b) in enumerate((
        (uv_hbm, uv_v.at[:, uvc]),
        (wo_hbm.at[:, pl.ds(other, COLS)], wo_v.at[pl.ds(pl.multiple_of(c * 128, 128), 128), :]),
        (wg_hbm.at[pl.ds(other, COLS), :], w_v.at[c, 0]),
        (wu_hbm.at[pl.ds(other, COLS), :], w_v.at[c, 1]),
        (wd_hbm.at[:, pl.ds(other, COLS)], wd_v.at[c]),
        (res_ref, res_v.at[c]),
        (cf_v.at[c], cf_v.at[c]),
    ))]
    for i in (0, 1, 5, 6, 2, 3, 4):
        early[i].start()
    for cp in local[3:6]:
        cp.start()

    for i in (0, 1, 2):
        local[i].wait()
    for i in (0, 1):
        early[i].wait_recv()

    @pl.loop(1, 64)
    def _(i):
        k, to = peer(i)
        remote(o_ref.at[k], x_v.at[k], a_ss.at[i], a_rs.at[k], to).wait_recv()

    m = jnp.dot(x_v.reshape(512, 512)[...], uv_v[...], preferred_element_type=f32)
    row = lax.broadcasted_iota(jnp.int32, (512, 256), 0)
    col = lax.broadcasted_iota(jnp.int32, (512, 256), 1)
    m = jnp.where((row // 4) % 2 == col // 128, m, 0.0).astype(bf)
    t = lax.broadcasted_iota(jnp.int32, (512, 512), 0)
    r = lax.broadcasted_iota(jnp.int32, (512, 512), 1)
    put = jnp.where((t // 8 == r // 8) & (t % 4 == r % 4) & ((t // 4) % 2 == c), 1.0, 0.0).astype(bf)
    hs_v[0] = jnp.dot(put, m, preferred_element_type=f32).astype(bf)
    swap = remote(hs_v.at[0], hs_v.at[1], s_ss.at[0], s_rs.at[0], sib)
    swap.start()
    swap.wait()
    h_v[...] = hs_v[0] + hs_v[1]
    acc2 = acc.reshape(512, COLS)

    @pl.loop(0, 7)
    def _(i):
        cols = pl.ds(pl.multiple_of(i * 512, 512), 512)
        acc2[:, cols] = jnp.dot(h_v[...], wo_v[:, cols], preferred_element_type=f32).astype(bf)

    reduce_scatter(pos, c, acc, (b0, b1, b2), r1_ss, r1_rs, part.at[0])
    swap = remote(part.at[0], part.at[1], s_ss.at[1], s_rs.at[1], sib)
    swap.start()
    local[6].wait()
    early[5].wait_recv()
    early[6].wait_recv()
    res8 = lambda cols: jnp.concatenate([res_v[0, :, cols].astype(f32), res_v[1, :, cols].astype(f32)], axis=0)
    swap.wait()
    part[0] += res8(pl.ds(mine, COLS))
    part[1] += res8(pl.ds(other, COLS))
    squares = jnp.sum(part[0] * part[0], axis=1, keepdims=True) + jnp.sum(part[1] * part[1], axis=1, keepdims=True)
    scale = lax.rsqrt(squares * (1.0 / (2 * COLS)) + 1e-06)
    gmine = g_v.at[z, x, y]
    gmine[:, :COLS] = (part[0] * scale * gain_ref[:, pl.ds(mine, COLS)].astype(f32)).astype(bf)
    gmine[:, COLS:] = jnp.concatenate([cf_v[0], cf_v[1]], axis=0).astype(bf)

    all_gather(pos, c, g_v, g_ss, g_rs)

    for i in (3, 4, 5):
        local[i].wait()
    for i in (2, 3, 4):
        early[i].wait_recv()
    tokens = g_v.reshape(512, GCOLS)

    def product(which, gu):
        return jnp.dot(tokens[:, :COLS], w_v[which, gu], preferred_element_type=f32)

    for gu in (0, 1):
        snd_v[gu] = product(1 - c, gu).astype(bf)
    swap = remote(snd_v, rcv_v, s_ss.at[2], s_rs.at[2], sib)
    swap.start()
    coefs = tokens[:, COLS:].astype(f32)
    lane = lax.broadcasted_iota(jnp.int32, (512, 128), 1)
    column = jnp.sum(jnp.where((lane % 32 == e) & (lane < 64), coefs, 0.0), axis=1, keepdims=True)
    gate = product(c, 0)
    up = product(c, 1)
    swap.wait()
    gate += rcv_v[0].astype(f32)
    up += rcv_v[1].astype(f32)
    act_v[c] = (gate / (1.0 + jnp.exp(-gate)) * up * column).astype(bf)
    swap = remote(act_v.at[c], act_v.at[c], s_ss.at[3], s_rs.at[3], sib)
    swap.start()
    swap.wait()

    @pl.loop(0, 7)
    def _(i):
        cols = pl.ds(pl.multiple_of(i * 512, 512), 512)
        acc2[:, cols] = (jnp.dot(act_v[0], wd_v[0, :, cols], preferred_element_type=f32)
                         + jnp.dot(act_v[1], wd_v[1, :, cols], preferred_element_type=f32)).astype(bf)

    reduce_scatter(pos, c, acc, (b0, b1, b2), r2_ss, r2_rs, part.at[2])
    fin_v[0] = part[2, 0:4, :]
    fin_v[1] = part[2, 4:8, :]
    swap = remote(fin_v.at[1 - c], fin_v.at[2], s_ss.at[4], s_rs.at[4], sib)
    swap.start()

    def own(v):
        return jnp.where(c == 0, v[0:4, :], v[4:8, :])
    out_ref[:, pl.ds(mine, COLS)] = (own(part[0]) + fin_v[c]).astype(bf)
    swap.wait()
    out_ref[:, pl.ds(other, COLS)] = (own(part[1]) + fin_v[2]).astype(bf)

    @pl.loop(1, 64)
    def _(i):
        k, to = peer(i)
        remote(o_ref.at[k], x_v.at[k], a_ss.at[i], a_rs.at[k], to).wait_send()
    for cp in early:
        cp.wait_send()


def layer_call(o, ids, scores, residual, gain, uv, wo, wg, wu, wd):
    vm = pl.BlockSpec(memory_space=pltpu.VMEM)
    hbm = pl.BlockSpec(memory_space=pl.ANY)
    dma = pltpu.SemaphoreType.DMA
    return pl.pallas_call(
        layer_kernel, out_shape=jax.ShapeDtypeStruct((4, 2 * COLS), bf),
        in_specs=[vm, vm, vm, vm, vm, hbm, hbm, hbm, hbm, hbm], out_specs=vm,
        scratch_shapes=[
            pltpu.VMEM((64, 8, 512), bf), pltpu.VMEM((512, 256), bf), pltpu.VMEM((256, COLS), bf), pltpu.VMEM((2, 2, COLS, 256), bf),
            pltpu.VMEM((2, 256, COLS), bf), pltpu.VMEM((512, 256), bf), pltpu.VMEM((2, 512, 256), bf),
            pltpu.VMEM((4, 4, 4, 8, COLS), bf), pltpu.VMEM((4, 4, 4, 8, COLS), bf), pltpu.VMEM((3, 4, 8, COLS), bf), pltpu.VMEM((3, 8, COLS), bf),
            pltpu.VMEM((3, 8, COLS), f32), pltpu.VMEM((2, 4, 2 * COLS), bf), pltpu.VMEM((2, 4, 128), f32), pltpu.VMEM((4, 4, 4, 8, GCOLS), bf),
            pltpu.VMEM((2, 512, 256), bf), pltpu.VMEM((2, 512, 256), bf), pltpu.VMEM((2, 512, 256), bf), pltpu.VMEM((3, 4, COLS), f32),
            dma((64,)), dma((64,)), dma((7,)), dma((7,)), dma((7,)), dma((5,)), dma((5,)),
            dma((3, 10)), dma((3, 10)), dma((3, 10)), dma((3, 10)), dma((3, 10)), dma((3, 10))],
        compiler_params=pltpu.CompilerParams(collective_id=1, has_side_effects=True, vmem_limit_bytes=56 << 20),
    )(o, ids, scores, residual, gain, uv, wo, wg, wu, wd)

LAT=512; KV=576; HEADS=128; STEPS=4; CACHE=8192
LOG2E=1.4426950408889634
SCALE=(192.0)**-0.5
f32=jnp.float32; bf=jnp.bfloat16

def attn_kernel(T, RB, len_ref, qt_ref, new_ref, kt_ref, o_ref, q_sc, kbuf, m_sc, l_sc, acc_sc, sem):
    n = len_ref[0]
    nblk = (n + T - 1) // T
    ROWS = STEPS*HEADS
    c = SCALE*LOG2E

    def fetch(i, slot):
        return pltpu.make_async_copy(kt_ref.at[:, pl.ds(pl.multiple_of(i*T, T), T)], kbuf.at[slot], sem.at[slot])
    fetch(0, 0).start()
    for s in range(STEPS):
        q_sc[s*HEADS:(s+1)*HEADS, :] = qt_ref[s].T
    for s in range(STEPS):
        q = q_sc[s*HEADS:(s+1)*HEADS, :]
        sc = lax.dot_general(q, new_ref[...], (((1,),(1,)),((),())), preferred_element_type=f32) * c
        col = lax.broadcasted_iota(jnp.int32, sc.shape, 1)
        sc = jnp.where(col <= s, sc, -1e30)
        m = jnp.max(sc, axis=1, keepdims=True)
        p = jnp.exp2(sc - m)
        l = jnp.sum(p, axis=1, keepdims=True)
        m_sc[s*HEADS:(s+1)*HEADS, :] = jnp.broadcast_to(m, (HEADS, 128))
        l_sc[s*HEADS:(s+1)*HEADS, :] = jnp.broadcast_to(l, (HEADS, 128))
        acc_sc[s*HEADS:(s+1)*HEADS, :] = jnp.dot(p.astype(bf), new_ref[:, :LAT], preferred_element_type=f32)

    def block(i, masked):
        slot = lax.rem(i, 2)
        fetch(i, slot).wait()
        @pl.when(i + 1 < nblk)
        def _():
            fetch(i + 1, 1 - slot).start()
        kt = kbuf.at[slot]
        for r in range(0, ROWS, RB):
            s_ = jnp.dot(q_sc[r:r+RB, :], kt[...], preferred_element_type=f32)
            if masked:
                col = lax.broadcasted_iota(jnp.int32, (1, T), 1) + i*T
                s_ = jnp.where(col < n, s_, -1e30)
            mo = m_sc[r:r+RB, :1]
            mn = jnp.maximum(mo, jnp.max(s_, axis=1, keepdims=True) * c)
            a = jnp.exp2(mo - mn)
            p = jnp.exp2(s_ * c - mn)
            l_sc[r:r+RB, :] = l_sc[r:r+RB, :] * a + jnp.sum(p, axis=1, keepdims=True)
            pv = lax.dot_general(p.astype(bf), kt[:LAT, :], (((1,),(1,)),((),())), preferred_element_type=f32)
            acc_sc[r:r+RB, :] = acc_sc[r:r+RB, :] * a + pv
            m_sc[r:r+RB, :] = jnp.broadcast_to(mn, (RB, 128))
    nfull = n // T
    @pl.loop(0, nfull)
    def _(i):
        block(i, False)
    @pl.when(nfull < nblk)
    def _():
        block(nfull, True)
    ob = (acc_sc[...] * (1.0 / l_sc[:, :1])).astype(bf)
    i0 = lax.broadcasted_iota(jnp.int32, (ROWS, ROWS), 0)
    i1 = lax.broadcasted_iota(jnp.int32, (ROWS, ROWS), 1)
    perm = jnp.where((i0 % 4) * HEADS + i0 // 4 == i1, 1.0, 0.0).astype(bf)
    o_ref[...] = jnp.dot(perm, ob, preferred_element_type=f32).astype(bf)

def attend(queries, new_latent, cache_latent, cache_len, T=1024, RB=256):
    qt = jnp.swapaxes(queries[0], 1, 2)
    kt = jnp.swapaxes(cache_latent[0], 0, 1)
    new = jnp.pad(new_latent[0], ((0, 128 - STEPS), (0, 0)))
    return pl.pallas_call(
        functools.partial(attn_kernel, T, RB),
        out_shape=jax.ShapeDtypeStruct((STEPS*HEADS, LAT), bf),
        in_specs=[pl.BlockSpec(memory_space=pltpu.SMEM), pl.BlockSpec(memory_space=pltpu.VMEM), pl.BlockSpec(memory_space=pltpu.VMEM), pl.BlockSpec(memory_space=pl.ANY)],
        out_specs=pl.BlockSpec(memory_space=pltpu.VMEM),
        scratch_shapes=[pltpu.VMEM((STEPS*HEADS, KV), bf), pltpu.VMEM((2, KV, T), bf), pltpu.VMEM((STEPS*HEADS, 128), f32), pltpu.VMEM((STEPS*HEADS, 128), f32),
                        pltpu.VMEM((STEPS*HEADS, LAT), f32), pltpu.SemaphoreType.DMA((2,))],
        compiler_params=pltpu.CompilerParams(vmem_limit_bytes=48 << 20),
    )(cache_len, qt, new, kt)

def per_device(queries, new_latent, cache_latent, cache_len, route_ids, route_scores, residual, norm_gain,
               w_uv, w_out, w_gate, w_up, w_down):
    latent = attend(queries, new_latent, cache_latent, cache_len)
    return layer_call(latent.reshape(64, 8, 512), route_ids[0], route_scores[0], residual[0], norm_gain[None],
                      w_uv[0], w_out[0], w_gate[0], w_up[0], w_down[0])[None]


def solution(mesh):
    r = ("sec", "ep")
    placed = (P(r, None, None, None), P(r, None, None), P(r, None, None), P(r), P(r, None, None), P(r, None, None), P(r, None, None),
              P(), P(r, None, None), P(r, None, None), P("ep", None, "sec"), P("ep", None, "sec"), P("ep", "sec", None))
    return jax.shard_map(per_device, mesh=mesh, in_specs=placed, out_specs=P(r, None, None), check_vma=False)
```

```python
import functools
import jax, jax.numpy as jnp
from jax import lax
from jax.experimental import pallas as pl
from jax.experimental.pallas import tpu as pltpu
from jax.sharding import PartitionSpec as P

MESH = pl.DeviceIdType.MESH
f32 = jnp.float32
bf = jnp.bfloat16
COLS = 3584
GCOLS = 3712
ORDERS = ((0, 1, 2), (1, 2, 0), (2, 0, 1))


def streams(groups):
    start, made = 0, []
    for tiles, halves in groups:
        made.append([])
        for p in range(3):
            made[-1].append((start, tiles[p] * 128, halves[p] * 128, ORDERS[p]))
            start += tiles[p] * 128
    return made


RS = streams((((5, 5, 4), (3, 3, 2)), ((5, 4, 5), (2, 2, 2))))
AG = streams((((5, 5, 4), (3, 3, 2)), ((5, 5, 5), (2, 2, 3))))
GROUPS = len(RS)
WIDTH = COLS // GROUPS


def dev(pos, c):
    return (pos[0], (pos[1] * 4 + pos[2]) * 2 + c)


def shifted(pos, axis, by):
    out = list(pos)
    out[axis] = (pos[axis] + by) % 4
    return tuple(out)


def remote(src, dst, ss, rs, to):
    return pltpu.make_async_remote_copy(src_ref=src, dst_ref=dst, send_sem=ss, recv_sem=rs, device_id=to, device_id_type=MESH)


def region(pos, stream, stage, q, lo=0, hi=None):
    start, width, _, order = stream
    idx = [slice(None)] * 3
    for k in range(stage):
        idx[order[k]] = pos[order[k]]
    idx[order[stage]] = q
    return tuple(idx) + (slice(None), slice(start + lo, start + (width if hi is None else hi)))


def halves(stream):
    _, width, half, _ = stream
    return ((0, 1, 0, half), (1, 3, half, width))


class ReduceScatter:
    def __init__(self, pos, c, acc, bufs, ss, rs, out):
        self.pos, self.c, self.acc, self.bufs, self.ss, self.rs, self.out = pos, c, acc, bufs, ss, rs, out
        self.copies = {}

    def reg(self, st, stage, q, lo=0, hi=None):
        return self.acc.at[region(self.pos, st, stage, q, lo, hi)]

    def slot(self, st, stage, d, lo=0, hi=None):
        start, width = st[:2]
        return self.bufs[stage].at[(d,) + (slice(None),) * (2 - stage) + (slice(None), slice(start + lo, start + (width if hi is None else hi)))]

    def send(self, g, p, n, src, dst, axis, by):
        cp = remote(src, dst, self.ss.at[g, p, n], self.rs.at[g, p, n], dev(shifted(self.pos, axis, by), self.c))
        cp.start()
        self.copies[g, p, n] = cp

    def total(self, g, p, st, stage, first, count):
        axis = st[3][stage]
        total = self.reg(st, stage, self.pos[axis])[...].astype(f32)
        for d in range(count):
            self.copies[g, p, first + d].wait_recv()
            total += self.slot(st, stage, d)[...].astype(f32)
        return total

    def step(self, g, k):
        pos = self.pos
        for p, st in enumerate(RS[g]):
            start, width, _, order = st
            if k == 0:
                for d, by, lo, hi in halves(st):
                    self.send(g, p, d, self.reg(st, 0, (pos[order[0]] + 2) % 4, lo, hi), self.slot(st, 0, 2 + d, lo, hi), order[0], by)
            elif k == 1:
                for d, by, lo, hi in halves(st):
                    q = (pos[order[0]] + by) % 4
                    self.copies[g, p, d].wait_recv()
                    dst = self.reg(st, 0, q, lo, hi)
                    dst[...] = (dst[...].astype(f32) + self.slot(st, 0, 2 + d, lo, hi)[...].astype(f32)).astype(bf)
                for d, by in ((0, 1), (1, 3)):
                    q = (pos[order[0]] + by) % 4
                    self.send(g, p, 2 + d, self.reg(st, 0, q), self.slot(st, 0, d), order[0], by)
            elif k in (2, 3):
                stage = k - 1
                mine = self.reg(st, stage - 1, pos[order[stage - 1]])
                mine[...] = (self.total(g, p, st, 0, 2, 2) if k == 2 else self.total(g, p, st, 1, 4, 3)).astype(bf)
                for by in (1, 2, 3):
                    q = (pos[order[stage]] + by) % 4
                    self.send(g, p, 1 + 3 * stage + by - 1, self.reg(st, stage, q), self.slot(st, stage, by - 1), order[stage], by)
            else:
                self.out[:, start:start + width] = self.total(g, p, st, 2, 7, 3)

    def drain(self):
        for cp in self.copies.values():
            cp.wait_send()


class AllGather:
    def __init__(self, pos, c, g, ss, rs):
        self.pos, self.c, self.g, self.ss, self.rs = pos, c, g, ss, rs
        self.copies = {}

    def send(self, g, p, n, st, stage, q, lo, hi, axis, by):
        r = self.g.at[region(self.pos, st, stage, q, lo, hi)]
        cp = remote(r, r, self.ss.at[g, p, n], self.rs.at[g, p, n], dev(shifted(self.pos, axis, by), self.c))
        cp.start()
        self.copies[g, p, n] = cp

    def arrived(self, g, p, *which):
        for n in which:
            self.copies[g, p, n].wait_recv()

    def step(self, g, k):
        pos = self.pos
        for p, st in enumerate(AG[g]):
            order = st[3]
            if k in (0, 1):
                stage = 2 - k
                if k == 1:
                    self.arrived(g, p, 7, 8, 9)
                for by in (1, 2, 3):
                    self.send(g, p, 1 + 3 * stage + by - 1, st, stage, pos[order[stage]], 0, None, order[stage], by)
            elif k == 2:
                self.arrived(g, p, 4, 5, 6)
                for d, by in ((0, 1), (1, 3)):
                    self.send(g, p, d, st, 0, pos[order[0]], 0, None, order[0], by)
            elif k == 3:
                for d, by, lo, hi in halves(st):
                    self.arrived(g, p, d)
                    self.send(g, p, 2 + d, st, 0, (pos[order[0]] + 4 - by) % 4, lo, hi, order[0], by)
            else:
                self.arrived(g, p, 2, 3)

    def drain(self):
        for cp in self.copies.values():
            cp.wait_send()


def layer_kernel(o_ref, ids_ref, sc_ref, res_ref, gain_ref, uv_hbm, wo_hbm, wg_hbm, wu_hbm, wd_hbm, out_ref,
                 x_v, uv_v, wo_v, w_v, wd_v, h_v, hs_v, acc, b0, b1, b2, part, res_v, cf_v, g_v, gu_v, snd_v, rcv_v, act_v, fin_v,
                 a_ss, a_rs, l_sem, w_ss, w_rs, s_ss, s_rs, r1_ss, r1_rs, g_ss, g_rs, r2_ss, r2_rs):
    z = lax.axis_index("sec")
    e = lax.axis_index("ep")
    x, y, c = e // 8, (e // 2) % 4, e % 2
    pos = (z, x, y)
    me = z * 16 + x * 4 + y
    sib = dev(pos, 1 - c)
    mine = pl.multiple_of(c * COLS, 128)
    other = pl.multiple_of((1 - c) * COLS, 128)

    def peer(i):
        k = (me + i) % 64
        return k, (k // 16, (k % 16) * 2 + c)

    barrier = pltpu.get_barrier_semaphore()

    @pl.loop(1, 64)
    def _(i):
        pl.semaphore_signal(barrier, inc=1, device_id=peer(i)[1], device_id_type=MESH)
    pl.semaphore_signal(barrier, inc=1, device_id=sib, device_id_type=MESH)

    uvc = pl.ds(pl.multiple_of(c * 128, 128), 128)
    local = [pltpu.make_async_copy(a, b, l_sem.at[i]) for i, (a, b) in enumerate((
        (o_ref.at[me], x_v.at[me]),
        (uv_hbm, uv_v.at[:, uvc]),
        (wo_hbm.at[:, pl.ds(mine, COLS)], wo_v.at[pl.ds(pl.multiple_of(c * 128, 128), 128), :]),
        (wg_hbm.at[pl.ds(mine, COLS), :], w_v.at[c, 0]),
        (wu_hbm.at[pl.ds(mine, COLS), :], w_v.at[c, 1]),
        (wd_hbm.at[:, pl.ds(mine, COLS)], wd_v.at[pl.ds(pl.multiple_of(c * 256, 256), 256), :]),
        (res_ref, res_v.at[c]),
    ))]
    for cp in local[:3]:
        cp.start()
    local[6].start()
    sc = sc_ref[...]
    shares = sc / jnp.sum(sc, axis=1, keepdims=True) * 2.5
    ids = ids_ref[...]
    lane = lax.broadcasted_iota(jnp.int32, (4, 128), 1)
    coef = jnp.zeros((4, 128), f32)
    for k in range(8):
        coef += jnp.where(lane % 32 == ids[:, k:k + 1], shares[:, k:k + 1], 0.0)
    high = coef.astype(bf).astype(f32)
    cf_v[c] = jnp.where(lane < 32, high, jnp.where(lane < 64, coef - high, 0.0))

    pl.semaphore_wait(barrier, 64)

    @pl.loop(1, 64)
    def _(i):
        k, to = peer(i)
        remote(o_ref.at[k], x_v.at[me], a_ss.at[i], a_rs.at[me], to).start()

    early = [remote(a, b, w_ss.at[i], w_rs.at[i], sib) for i, (a, b) in enumerate((
        (uv_hbm, uv_v.at[:, uvc]),
        (wo_hbm.at[:, pl.ds(other, COLS)], wo_v.at[pl.ds(pl.multiple_of(c * 128, 128), 128), :]),
        (wg_hbm.at[pl.ds(other, COLS), :], w_v.at[c, 0]),
        (wu_hbm.at[pl.ds(other, COLS), :], w_v.at[c, 1]),
        (wd_hbm.at[:, pl.ds(other, COLS)], wd_v.at[pl.ds(pl.multiple_of(c * 256, 256), 256), :]),
        (res_ref, res_v.at[c]),
        (cf_v.at[c], cf_v.at[c]),
    ))]
    for i in (0, 1, 5, 6, 2, 3, 4):
        early[i].start()
    for cp in local[3:6]:
        cp.start()

    for i in (0, 1, 2):
        local[i].wait()
    for i in (0, 1):
        early[i].wait_recv()

    @pl.loop(1, 64)
    def _(i):
        k, to = peer(i)
        remote(o_ref.at[k], x_v.at[k], a_ss.at[i], a_rs.at[k], to).wait_recv()

    m = jnp.dot(x_v.reshape(512, 512)[...], uv_v[...], preferred_element_type=f32)
    row = lax.broadcasted_iota(jnp.int32, (512, 256), 0)
    col = lax.broadcasted_iota(jnp.int32, (512, 256), 1)
    m = jnp.where((row // 4) % 2 == col // 128, m, 0.0).astype(bf)
    t = lax.broadcasted_iota(jnp.int32, (512, 512), 0)
    r = lax.broadcasted_iota(jnp.int32, (512, 512), 1)
    put = jnp.where((t // 8 == r // 8) & (t % 4 == r % 4) & ((t // 4) % 2 == c), 1.0, 0.0).astype(bf)
    hs_v[0] = jnp.dot(put, m, preferred_element_type=f32).astype(bf)
    swap = remote(hs_v.at[0], hs_v.at[1], s_ss.at[0], s_rs.at[0], sib)
    swap.start()
    swap.wait()
    h_v[...] = hs_v[0] + hs_v[1]
    acc2 = acc.reshape(512, COLS)

    def project(a, w, g):
        for half in range(2):
            cols = slice(g * WIDTH + half * (WIDTH // 2), g * WIDTH + (half + 1) * (WIDTH // 2))
            acc2[:, cols] = jnp.dot(a[...], w[:, cols], preferred_element_type=f32).astype(bf)

    def project_and_reduce(a, w, ss, rs, out):
        sums = ReduceScatter(pos, c, acc, (b0, b1, b2), ss, rs, out)
        for k in range(5):
            for g in range(GROUPS):
                if k == 0:
                    project(a, w, g)
                sums.step(g, k)
        sums.drain()

    project_and_reduce(h_v, wo_v, r1_ss, r1_rs, part.at[0])
    swap = remote(part.at[0], part.at[1], s_ss.at[1], s_rs.at[1], sib)
    swap.start()
    local[6].wait()
    early[5].wait_recv()
    early[6].wait_recv()
    res8 = lambda cols: jnp.concatenate([res_v[0, :, cols].astype(f32), res_v[1, :, cols].astype(f32)], axis=0)
    swap.wait()
    part[0] += res8(pl.ds(mine, COLS))
    part[1] += res8(pl.ds(other, COLS))
    squares = jnp.sum(part[0] * part[0], axis=1, keepdims=True) + jnp.sum(part[1] * part[1], axis=1, keepdims=True)
    scale = lax.rsqrt(squares * (1.0 / (2 * COLS)) + 1e-06)
    gmine = g_v.at[z, x, y]
    gmine[:, :COLS] = (part[0] * scale * gain_ref[:, pl.ds(mine, COLS)].astype(f32)).astype(bf)
    gmine[:, COLS:] = jnp.concatenate([cf_v[0], cf_v[1]], axis=0).astype(bf)

    gather = AllGather(pos, c, g_v, g_ss, g_rs)
    tokens = g_v.reshape(512, GCOLS)
    for k in range(4):
        for g in range(GROUPS):
            gather.step(g, k)
    for i in (3, 4):
        local[i].wait()
    for i in (2, 3):
        early[i].wait_recv()

    def product(which, gu, g):
        rows = slice(g * WIDTH, (g + 1) * WIDTH)
        return jnp.dot(tokens[:, rows], w_v[which, gu, rows, :], preferred_element_type=f32)

    for g in range(GROUPS):
        gather.step(g, 4)
        for n, which in ((0, 1 - c), (1, c)):
            for gu in (0, 1):
                new = product(which, gu, g)
                if g > 0:
                    new += gu_v[n, gu]
                if g < GROUPS - 1:
                    gu_v[n, gu] = new
                elif n == 0:
                    snd_v[gu] = new.astype(bf)
                else:
                    gu_v[n, gu] = new
            if n == 0 and g == GROUPS - 1:
                swap = remote(snd_v, rcv_v, s_ss.at[2], s_rs.at[2], sib)
                swap.start()
    coefs = tokens[:, COLS:].astype(f32)
    lane = lax.broadcasted_iota(jnp.int32, (512, 128), 1)
    column = jnp.sum(jnp.where((lane % 32 == e) & (lane < 64), coefs, 0.0), axis=1, keepdims=True)
    swap.wait()
    gate = gu_v[1, 0] + rcv_v[0].astype(f32)
    up = gu_v[1, 1] + rcv_v[1].astype(f32)
    acts = act_v.at[:, pl.ds(pl.multiple_of(c * 256, 256), 256)]
    acts[...] = (gate / (1.0 + jnp.exp(-gate)) * up * column).astype(bf)
    swap = remote(acts, acts, s_ss.at[3], s_rs.at[3], sib)
    swap.start()
    local[5].wait()
    early[4].wait_recv()
    swap.wait()
    project_and_reduce(act_v, wd_v, r2_ss, r2_rs, part.at[2])
    fin_v[0] = part[2, 0:4, :]
    fin_v[1] = part[2, 4:8, :]
    swap = remote(fin_v.at[1 - c], fin_v.at[2], s_ss.at[4], s_rs.at[4], sib)
    swap.start()

    def own(v):
        return jnp.where(c == 0, v[0:4, :], v[4:8, :])
    out_ref[:, pl.ds(mine, COLS)] = (own(part[0]) + fin_v[c]).astype(bf)
    swap.wait()
    out_ref[:, pl.ds(other, COLS)] = (own(part[1]) + fin_v[2]).astype(bf)

    @pl.loop(1, 64)
    def _(i):
        k, to = peer(i)
        remote(o_ref.at[k], x_v.at[k], a_ss.at[i], a_rs.at[k], to).wait_send()
    for cp in early:
        cp.wait_send()
    gather.drain()


def layer_call(o, ids, scores, residual, gain, uv, wo, wg, wu, wd):
    vm = pl.BlockSpec(memory_space=pltpu.VMEM)
    hbm = pl.BlockSpec(memory_space=pl.ANY)
    dma = pltpu.SemaphoreType.DMA
    return pl.pallas_call(
        layer_kernel, out_shape=jax.ShapeDtypeStruct((4, 2 * COLS), bf),
        in_specs=[vm, vm, vm, vm, vm, hbm, hbm, hbm, hbm, hbm], out_specs=vm,
        scratch_shapes=[
            pltpu.VMEM((64, 8, 512), bf), pltpu.VMEM((512, 256), bf), pltpu.VMEM((256, COLS), bf), pltpu.VMEM((2, 2, COLS, 256), bf),
            pltpu.VMEM((512, COLS), bf), pltpu.VMEM((512, 256), bf), pltpu.VMEM((2, 512, 256), bf),
            pltpu.VMEM((4, 4, 4, 8, COLS), bf), pltpu.VMEM((4, 4, 4, 8, COLS), bf), pltpu.VMEM((3, 4, 8, COLS), bf), pltpu.VMEM((3, 8, COLS), bf),
            pltpu.VMEM((3, 8, COLS), f32), pltpu.VMEM((2, 4, 2 * COLS), bf), pltpu.VMEM((2, 4, 128), f32), pltpu.VMEM((4, 4, 4, 8, GCOLS), bf),
            pltpu.VMEM((2, 2, 512, 256), f32), pltpu.VMEM((2, 512, 256), bf), pltpu.VMEM((2, 512, 256), bf), pltpu.VMEM((512, 512), bf), pltpu.VMEM((3, 4, COLS), f32),
            dma((64,)), dma((64,)), dma((7,)), dma((7,)), dma((7,)), dma((5,)), dma((5,)),
            *[dma((GROUPS, 3, 10)) for _ in range(6)]],
        compiler_params=pltpu.CompilerParams(collective_id=1, has_side_effects=True, vmem_limit_bytes=56 << 20),
    )(o, ids, scores, residual, gain, uv, wo, wg, wu, wd)

LAT=512; KV=576; HEADS=128; STEPS=4; CACHE=8192
LOG2E=1.4426950408889634
SCALE=(192.0)**-0.5
f32=jnp.float32; bf=jnp.bfloat16

def attn_kernel(T, RB, len_ref, qt_ref, new_ref, kt_ref, o_ref, q_sc, kbuf, m_sc, l_sc, acc_sc, sem):
    n = len_ref[0]
    nblk = (n + T - 1) // T
    ROWS = STEPS*HEADS
    c = SCALE*LOG2E

    def fetch(i, slot):
        return pltpu.make_async_copy(kt_ref.at[:, pl.ds(pl.multiple_of(i*T, T), T)], kbuf.at[slot], sem.at[slot])
    fetch(0, 0).start()
    for s in range(STEPS):
        q_sc[s*HEADS:(s+1)*HEADS, :] = qt_ref[s].T
    for s in range(STEPS):
        q = q_sc[s*HEADS:(s+1)*HEADS, :]
        sc = lax.dot_general(q, new_ref[...], (((1,),(1,)),((),())), preferred_element_type=f32) * c
        col = lax.broadcasted_iota(jnp.int32, sc.shape, 1)
        sc = jnp.where(col <= s, sc, -1e30)
        m = jnp.max(sc, axis=1, keepdims=True)
        p = jnp.exp2(sc - m)
        l = jnp.sum(p, axis=1, keepdims=True)
        m_sc[s*HEADS:(s+1)*HEADS, :] = jnp.broadcast_to(m, (HEADS, 128))
        l_sc[s*HEADS:(s+1)*HEADS, :] = jnp.broadcast_to(l, (HEADS, 128))
        acc_sc[s*HEADS:(s+1)*HEADS, :] = jnp.dot(p.astype(bf), new_ref[:, :LAT], preferred_element_type=f32)

    def block(i, masked):
        slot = lax.rem(i, 2)
        fetch(i, slot).wait()
        @pl.when(i + 1 < nblk)
        def _():
            fetch(i + 1, 1 - slot).start()
        kt = kbuf.at[slot]
        for r in range(0, ROWS, RB):
            s_ = jnp.dot(q_sc[r:r+RB, :], kt[...], preferred_element_type=f32)
            if masked:
                col = lax.broadcasted_iota(jnp.int32, (1, T), 1) + i*T
                s_ = jnp.where(col < n, s_, -1e30)
            mo = m_sc[r:r+RB, :1]
            mn = jnp.maximum(mo, jnp.max(s_, axis=1, keepdims=True) * c)
            a = jnp.exp2(mo - mn)
            p = jnp.exp2(s_ * c - mn)
            l_sc[r:r+RB, :] = l_sc[r:r+RB, :] * a + jnp.sum(p, axis=1, keepdims=True)
            pv = lax.dot_general(p.astype(bf), kt[:LAT, :], (((1,),(1,)),((),())), preferred_element_type=f32)
            acc_sc[r:r+RB, :] = acc_sc[r:r+RB, :] * a + pv
            m_sc[r:r+RB, :] = jnp.broadcast_to(mn, (RB, 128))
    nfull = n // T
    @pl.loop(0, nfull)
    def _(i):
        block(i, False)
    @pl.when(nfull < nblk)
    def _():
        block(nfull, True)
    ob = (acc_sc[...] * (1.0 / l_sc[:, :1])).astype(bf)
    i0 = lax.broadcasted_iota(jnp.int32, (ROWS, ROWS), 0)
    i1 = lax.broadcasted_iota(jnp.int32, (ROWS, ROWS), 1)
    perm = jnp.where((i0 % 4) * HEADS + i0 // 4 == i1, 1.0, 0.0).astype(bf)
    o_ref[...] = jnp.dot(perm, ob, preferred_element_type=f32).astype(bf)

def attend(queries, new_latent, cache_latent, cache_len, T=1024, RB=256):
    qt = jnp.swapaxes(queries[0], 1, 2)
    kt = jnp.swapaxes(cache_latent[0], 0, 1)
    new = jnp.pad(new_latent[0], ((0, 128 - STEPS), (0, 0)))
    return pl.pallas_call(
        functools.partial(attn_kernel, T, RB),
        out_shape=jax.ShapeDtypeStruct((STEPS*HEADS, LAT), bf),
        in_specs=[pl.BlockSpec(memory_space=pltpu.SMEM), pl.BlockSpec(memory_space=pltpu.VMEM), pl.BlockSpec(memory_space=pltpu.VMEM), pl.BlockSpec(memory_space=pl.ANY)],
        out_specs=pl.BlockSpec(memory_space=pltpu.VMEM),
        scratch_shapes=[pltpu.VMEM((STEPS*HEADS, KV), bf), pltpu.VMEM((2, KV, T), bf), pltpu.VMEM((STEPS*HEADS, 128), f32), pltpu.VMEM((STEPS*HEADS, 128), f32),
                        pltpu.VMEM((STEPS*HEADS, LAT), f32), pltpu.SemaphoreType.DMA((2,))],
        compiler_params=pltpu.CompilerParams(vmem_limit_bytes=48 << 20),
    )(cache_len, qt, new, kt)

def per_device(queries, new_latent, cache_latent, cache_len, route_ids, route_scores, residual, norm_gain,
               w_uv, w_out, w_gate, w_up, w_down):
    latent = attend(queries, new_latent, cache_latent, cache_len)
    return layer_call(latent.reshape(64, 8, 512), route_ids[0], route_scores[0], residual[0], norm_gain[None],
                      w_uv[0], w_out[0], w_gate[0], w_up[0], w_down[0])[None]


def solution(mesh):
    r = ("sec", "ep")
    placed = (P(r, None, None, None), P(r, None, None), P(r, None, None), P(r), P(r, None, None), P(r, None, None), P(r, None, None),
              P(), P(r, None, None), P(r, None, None), P("ep", None, "sec"), P("ep", None, "sec"), P("ep", "sec", None))
    return jax.shard_map(per_device, mesh=mesh, in_specs=placed, out_specs=P(r, None, None), check_vma=False)
```

```python
import functools
import jax, jax.numpy as jnp
from jax import lax
from jax.experimental import pallas as pl
from jax.experimental.pallas import tpu as pltpu
from jax.sharding import PartitionSpec as P

MESH = pl.DeviceIdType.MESH
f32 = jnp.float32
bf = jnp.bfloat16
COLS = 3584
GCOLS = 3712
ORDERS = ((0, 1, 2), (1, 2, 0), (2, 0, 1))


def streams(groups):
    start, made = 0, []
    for tiles, halves in groups:
        made.append([])
        for p in range(3):
            made[-1].append((start, tiles[p] * 128, halves[p] * 128, ORDERS[p]))
            start += tiles[p] * 128
    return made


RS = streams((((5, 5, 4), (3, 3, 2)), ((5, 4, 5), (2, 2, 2))))
AG = streams((((5, 5, 4), (3, 3, 2)), ((5, 5, 5), (2, 2, 3))))
GROUPS = len(RS)
WIDTH = COLS // GROUPS


def dev(pos, c):
    return (pos[0], (pos[1] * 4 + pos[2]) * 2 + c)


def shifted(pos, axis, by):
    out = list(pos)
    out[axis] = (pos[axis] + by) % 4
    return tuple(out)


def remote(src, dst, ss, rs, to):
    return pltpu.make_async_remote_copy(src_ref=src, dst_ref=dst, send_sem=ss, recv_sem=rs, device_id=to, device_id_type=MESH)


def region(pos, stream, stage, q, lo=0, hi=None):
    start, width, _, order = stream
    idx = [slice(None)] * 3
    for k in range(stage):
        idx[order[k]] = pos[order[k]]
    idx[order[stage]] = q
    return tuple(idx) + (slice(None), slice(start + lo, start + (width if hi is None else hi)))


def halves(stream):
    _, width, half, _ = stream
    return ((0, 1, 0, half), (1, 3, half, width))


class ReduceScatter:
    def __init__(self, pos, c, acc, bufs, ss, rs, out):
        self.pos, self.c, self.acc, self.bufs, self.ss, self.rs, self.out = pos, c, acc, bufs, ss, rs, out
        self.copies = {}

    def reg(self, st, stage, q, lo=0, hi=None):
        return self.acc.at[region(self.pos, st, stage, q, lo, hi)]

    def slot(self, st, stage, d, lo=0, hi=None):
        start, width = st[:2]
        return self.bufs[stage].at[(d,) + (slice(None),) * (2 - stage) + (slice(None), slice(start + lo, start + (width if hi is None else hi)))]

    def send(self, g, p, n, src, dst, axis, by):
        cp = remote(src, dst, self.ss.at[g, p, n], self.rs.at[g, p, n], dev(shifted(self.pos, axis, by), self.c))
        cp.start()
        self.copies[g, p, n] = cp

    def total(self, g, p, st, stage, first, count):
        axis = st[3][stage]
        total = self.reg(st, stage, self.pos[axis])[...].astype(f32)
        for d in range(count):
            self.copies[g, p, first + d].wait_recv()
            total += self.slot(st, stage, d)[...].astype(f32)
        return total

    def step(self, g, k):
        pos = self.pos
        for p, st in enumerate(RS[g]):
            start, width, _, order = st
            if k == 0:
                for d, by, lo, hi in halves(st):
                    self.send(g, p, d, self.reg(st, 0, (pos[order[0]] + 2) % 4, lo, hi), self.slot(st, 0, 2 + d, lo, hi), order[0], by)
            elif k == 1:
                for d, by, lo, hi in halves(st):
                    q = (pos[order[0]] + by) % 4
                    self.copies[g, p, d].wait_recv()
                    dst = self.reg(st, 0, q, lo, hi)
                    dst[...] = (dst[...].astype(f32) + self.slot(st, 0, 2 + d, lo, hi)[...].astype(f32)).astype(bf)
                for d, by in ((0, 1), (1, 3)):
                    q = (pos[order[0]] + by) % 4
                    self.send(g, p, 2 + d, self.reg(st, 0, q), self.slot(st, 0, d), order[0], by)
            elif k in (2, 3):
                stage = k - 1
                mine = self.reg(st, stage - 1, pos[order[stage - 1]])
                mine[...] = (self.total(g, p, st, 0, 2, 2) if k == 2 else self.total(g, p, st, 1, 4, 3)).astype(bf)
                for by in (1, 2, 3):
                    q = (pos[order[stage]] + by) % 4
                    self.send(g, p, 1 + 3 * stage + by - 1, self.reg(st, stage, q), self.slot(st, stage, by - 1), order[stage], by)
            else:
                self.out[:, start:start + width] = self.total(g, p, st, 2, 7, 3)

    def drain(self):
        for cp in self.copies.values():
            cp.wait_send()


class AllGather:
    def __init__(self, pos, c, g, ss, rs):
        self.pos, self.c, self.g, self.ss, self.rs = pos, c, g, ss, rs
        self.copies = {}

    def send(self, g, p, n, st, stage, q, lo, hi, axis, by):
        r = self.g.at[region(self.pos, st, stage, q, lo, hi)]
        cp = remote(r, r, self.ss.at[g, p, n], self.rs.at[g, p, n], dev(shifted(self.pos, axis, by), self.c))
        cp.start()
        self.copies[g, p, n] = cp

    def arrived(self, g, p, *which):
        for n in which:
            self.copies[g, p, n].wait_recv()

    def step(self, g, k):
        pos = self.pos
        for p, st in enumerate(AG[g]):
            order = st[3]
            if k in (0, 1):
                stage = 2 - k
                if k == 1:
                    self.arrived(g, p, 7, 8, 9)
                for by in (1, 2, 3):
                    self.send(g, p, 1 + 3 * stage + by - 1, st, stage, pos[order[stage]], 0, None, order[stage], by)
            elif k == 2:
                self.arrived(g, p, 4, 5, 6)
                for d, by in ((0, 1), (1, 3)):
                    self.send(g, p, d, st, 0, pos[order[0]], 0, None, order[0], by)
            elif k == 3:
                for d, by, lo, hi in halves(st):
                    self.arrived(g, p, d)
                    self.send(g, p, 2 + d, st, 0, (pos[order[0]] + 4 - by) % 4, lo, hi, order[0], by)
            else:
                self.arrived(g, p, 2, 3)

    def drain(self):
        for cp in self.copies.values():
            cp.wait_send()


T = 1024
KROWS = 592
SCORE = (192.0 ** -0.5) * 1.4426950408889634


def attention(len_ref, qt_ref, new_ref, kt_ref, q_sc, n_sc, kbuf, s_a, s_b, m_sc, l_sc, acc_sc, k_sem, between):
    blocks = kbuf.shape[0]
    copies = [pltpu.make_async_copy(kt_ref.at[:, i * T:(i + 1) * T], kbuf.at[i, 0:576, :], k_sem.at[i]) for i in range(blocks)]
    for cp in copies:
        cp.start()
    n = len_ref[0, 0]
    edge = lax.broadcasted_iota(jnp.int32, (16, T), 0)
    lane = lax.broadcasted_iota(jnp.int32, (16, T), 1)
    for i in range(blocks):
        kbuf[i, 576:592, :] = jnp.where((edge == 0) & (lane + i * T >= n), -1e30, 0.0).astype(bf)
    r0 = lax.broadcasted_iota(jnp.int32, (512, 512), 0)
    r1 = lax.broadcasted_iota(jnp.int32, (512, 512), 1)
    order = jnp.where((r0 % 4) * 128 + r0 // 4 == r1, 1.0, 0.0).astype(bf)
    q = jnp.concatenate([qt_ref[s].T for s in range(4)], axis=0)
    q_sc[:, 0:576] = jnp.dot(order, q, preferred_element_type=f32).astype(bf)
    q_sc[:, 576:592] = jnp.where(lax.broadcasted_iota(jnp.int32, (512, 16), 1) == 0, 1.0, 0.0).astype(bf)
    n_sc[...] = jnp.zeros_like(n_sc)
    n_sc[0:4, :] = new_ref[...]
    s = lax.dot_general(q_sc[:, 0:576], n_sc[...], (((1,), (1,)), ((), ())), preferred_element_type=f32) * SCORE
    row = lax.broadcasted_iota(jnp.int32, s.shape, 0)
    col = lax.broadcasted_iota(jnp.int32, s.shape, 1)
    s = jnp.where(col <= row % 4, s, -1e30)
    m = jnp.max(s, axis=1, keepdims=True)
    p = jnp.exp2(s - m)
    m_sc[...] = jnp.broadcast_to(m, (512, 128))
    l_sc[...] = jnp.broadcast_to(jnp.sum(p, axis=1, keepdims=True), (512, 128))
    acc_sc[...] = jnp.dot(p.astype(bf), n_sc[:, 0:512], preferred_element_type=f32)

    def scores(i, into):
        into[...] = jnp.dot(q_sc[...], kbuf[i], preferred_element_type=f32)

    def fold(i, s_ref):
        s = s_ref[...]
        old = m_sc[...]
        new = jnp.maximum(old, jnp.max(s, axis=1, keepdims=True) * SCORE)
        shrink = jnp.exp2(old - new)
        p = jnp.exp2(s * SCORE - new[:, 0:1])
        l_sc[...] = l_sc[...] * shrink + jnp.sum(p, axis=1, keepdims=True)
        m_sc[...] = new
        pv = lax.dot_general(p.astype(bf), kbuf[i, 0:512, :], (((1,), (1,)), ((), ())), preferred_element_type=f32)
        acc_sc[...] = acc_sc[...] * shrink[:, 0:1] + pv

    copies[0].wait()
    scores(0, s_a)
    for i in range(blocks):
        if i + 1 < blocks:
            copies[i + 1].wait()
            scores(i + 1, (s_a, s_b)[(i + 1) % 2])
        fold(i, (s_a, s_b)[i % 2])
        if i == 3:
            between()
    return acc_sc[...] * (1.0 / l_sc[:, 0:1])


def layer_kernel(len_ref, qt_ref, new_ref, kt_ref, ids_ref, sc_ref, res_ref, gain_ref, uv_hbm, wo_hbm, wg_hbm, wu_hbm, wd_hbm, out_ref,
                 q_sc, n_sc, kbuf, s_a, s_b, m_sc, l_sc, acc_sc, o_ref, x_v, uv_v, wo_v, w_v, wd_v, h_v, hs_v, acc, b0, b1, b2, part, res_v, cf_v, g_v, gu_v, snd_v, rcv_v, act_v, fin_v,
                 k_sem, a_ss, a_rs, l_sem, w_ss, w_rs, s_ss, s_rs, r1_ss, r1_rs, g_ss, g_rs, r2_ss, r2_rs):
    z = lax.axis_index("sec")
    e = lax.axis_index("ep")
    x, y, c = e // 8, (e // 2) % 4, e % 2
    pos = (z, x, y)
    me = z * 16 + x * 4 + y
    sib = dev(pos, 1 - c)
    mine = pl.multiple_of(c * COLS, 128)
    other = pl.multiple_of((1 - c) * COLS, 128)

    def peer(i):
        k = (me + i) % 64
        return k, (k // 16, (k % 16) * 2 + c)

    barrier = pltpu.get_barrier_semaphore()

    @pl.loop(1, 64)
    def _(i):
        pl.semaphore_signal(barrier, inc=1, device_id=peer(i)[1], device_id_type=MESH)
    pl.semaphore_signal(barrier, inc=1, device_id=sib, device_id_type=MESH)

    uvc = pl.ds(pl.multiple_of(c * 128, 128), 128)
    local = [pltpu.make_async_copy(a, b, l_sem.at[i]) for i, (a, b) in enumerate((
        (o_ref.at[me], x_v.at[me]),
        (uv_hbm, uv_v.at[:, uvc]),
        (wo_hbm.at[:, pl.ds(mine, COLS)], wo_v.at[pl.ds(pl.multiple_of(c * 128, 128), 128), :]),
        (wg_hbm.at[pl.ds(mine, COLS), :], w_v.at[c, 0]),
        (wu_hbm.at[pl.ds(mine, COLS), :], w_v.at[c, 1]),
        (wd_hbm.at[:, pl.ds(mine, COLS)], wd_v.at[pl.ds(pl.multiple_of(c * 256, 256), 256), :]),
        (res_ref, res_v.at[c]),
    ))]
    for i in (1, 2, 6):
        local[i].start()
    sc = sc_ref[...]
    shares = sc / jnp.sum(sc, axis=1, keepdims=True) * 2.5
    ids = ids_ref[...]
    lane = lax.broadcasted_iota(jnp.int32, (4, 128), 1)
    coef = jnp.zeros((4, 128), f32)
    for k in range(8):
        coef += jnp.where(lane % 32 == ids[:, k:k + 1], shares[:, k:k + 1], 0.0)
    high = coef.astype(bf).astype(f32)
    cf_v[c] = jnp.where(lane < 32, high, jnp.where(lane < 64, coef - high, 0.0))

    early = [remote(a, b, w_ss.at[i], w_rs.at[i], sib) for i, (a, b) in enumerate((
        (uv_hbm, uv_v.at[:, uvc]),
        (wo_hbm.at[:, pl.ds(other, COLS)], wo_v.at[pl.ds(pl.multiple_of(c * 128, 128), 128), :]),
        (wg_hbm.at[pl.ds(other, COLS), :], w_v.at[c, 0]),
        (wu_hbm.at[pl.ds(other, COLS), :], w_v.at[c, 1]),
        (wd_hbm.at[:, pl.ds(other, COLS)], wd_v.at[pl.ds(pl.multiple_of(c * 256, 256), 256), :]),
        (res_ref, res_v.at[c]),
        (cf_v.at[c], cf_v.at[c]),
    ))]
    def exchange_weights():
        pl.semaphore_wait(barrier, 64)
        for i in (0, 1, 5, 6, 2, 3, 4):
            early[i].start()
        for cp in local[3:6]:
            cp.start()

    latent = attention(len_ref, qt_ref, new_ref, kt_ref, q_sc, n_sc, kbuf, s_a, s_b, m_sc, l_sc, acc_sc, k_sem, exchange_weights)
    o_ref.reshape(512, 512)[...] = latent.astype(bf)
    local[0].start()

    @pl.loop(1, 64)
    def _(i):
        k, to = peer(i)
        remote(o_ref.at[k], x_v.at[me], a_ss.at[i], a_rs.at[me], to).start()

    for i in (0, 1, 2):
        local[i].wait()
    for i in (0, 1):
        early[i].wait_recv()

    @pl.loop(1, 64)
    def _(i):
        k, to = peer(i)
        remote(o_ref.at[k], x_v.at[k], a_ss.at[i], a_rs.at[k], to).wait_recv()

    m = jnp.dot(x_v.reshape(512, 512)[...], uv_v[...], preferred_element_type=f32)
    row = lax.broadcasted_iota(jnp.int32, (512, 256), 0)
    col = lax.broadcasted_iota(jnp.int32, (512, 256), 1)
    m = jnp.where((row // 4) % 2 == col // 128, m, 0.0).astype(bf)
    t = lax.broadcasted_iota(jnp.int32, (512, 512), 0)
    r = lax.broadcasted_iota(jnp.int32, (512, 512), 1)
    put = jnp.where((t // 8 == r // 8) & (t % 4 == r % 4) & ((t // 4) % 2 == c), 1.0, 0.0).astype(bf)
    hs_v[0] = jnp.dot(put, m, preferred_element_type=f32).astype(bf)
    swap = remote(hs_v.at[0], hs_v.at[1], s_ss.at[0], s_rs.at[0], sib)
    swap.start()
    swap.wait()
    h_v[...] = hs_v[0] + hs_v[1]
    acc2 = acc.reshape(512, COLS)

    def project(a, w, g):
        for half in range(2):
            cols = slice(g * WIDTH + half * (WIDTH // 2), g * WIDTH + (half + 1) * (WIDTH // 2))
            acc2[:, cols] = jnp.dot(a[...], w[:, cols], preferred_element_type=f32).astype(bf)

    def project_and_reduce(a, w, ss, rs, out):
        sums = ReduceScatter(pos, c, acc, (b0, b1, b2), ss, rs, out)
        for k in range(5):
            for g in range(GROUPS):
                if k == 0:
                    project(a, w, g)
                sums.step(g, k)
        sums.drain()

    project_and_reduce(h_v, wo_v, r1_ss, r1_rs, part.at[0])
    swap = remote(part.at[0], part.at[1], s_ss.at[1], s_rs.at[1], sib)
    swap.start()
    local[6].wait()
    early[5].wait_recv()
    early[6].wait_recv()
    res8 = lambda cols: jnp.concatenate([res_v[0, :, cols].astype(f32), res_v[1, :, cols].astype(f32)], axis=0)
    swap.wait()
    part[0] += res8(pl.ds(mine, COLS))
    part[1] += res8(pl.ds(other, COLS))
    squares = jnp.sum(part[0] * part[0], axis=1, keepdims=True) + jnp.sum(part[1] * part[1], axis=1, keepdims=True)
    scale = lax.rsqrt(squares * (1.0 / (2 * COLS)) + 1e-06)
    gmine = g_v.at[z, x, y]
    gmine[:, :COLS] = (part[0] * scale * gain_ref[:, pl.ds(mine, COLS)].astype(f32)).astype(bf)
    gmine[:, COLS:] = jnp.concatenate([cf_v[0], cf_v[1]], axis=0).astype(bf)

    gather = AllGather(pos, c, g_v, g_ss, g_rs)
    tokens = g_v.reshape(512, GCOLS)
    for k in range(4):
        for g in range(GROUPS):
            gather.step(g, k)
    for i in (3, 4):
        local[i].wait()
    for i in (2, 3):
        early[i].wait_recv()

    def product(which, gu, g):
        rows = slice(g * WIDTH, (g + 1) * WIDTH)
        return jnp.dot(tokens[:, rows], w_v[which, gu, rows, :], preferred_element_type=f32)

    for g in range(GROUPS):
        gather.step(g, 4)
        for n, which in ((0, 1 - c), (1, c)):
            for gu in (0, 1):
                new = product(which, gu, g)
                if g > 0:
                    new += gu_v[n, gu]
                if g < GROUPS - 1:
                    gu_v[n, gu] = new
                elif n == 0:
                    snd_v[gu] = new.astype(bf)
                else:
                    gu_v[n, gu] = new
            if n == 0 and g == GROUPS - 1:
                swap = remote(snd_v, rcv_v, s_ss.at[2], s_rs.at[2], sib)
                swap.start()
    coefs = tokens[:, COLS:].astype(f32)
    lane = lax.broadcasted_iota(jnp.int32, (512, 128), 1)
    column = jnp.sum(jnp.where((lane % 32 == e) & (lane < 64), coefs, 0.0), axis=1, keepdims=True)
    swap.wait()
    gate = gu_v[1, 0] + rcv_v[0].astype(f32)
    up = gu_v[1, 1] + rcv_v[1].astype(f32)
    acts = act_v.at[:, pl.ds(pl.multiple_of(c * 256, 256), 256)]
    acts[...] = (gate / (1.0 + jnp.exp(-gate)) * up * column).astype(bf)
    swap = remote(acts, acts, s_ss.at[3], s_rs.at[3], sib)
    swap.start()
    local[5].wait()
    early[4].wait_recv()
    swap.wait()
    project_and_reduce(act_v, wd_v, r2_ss, r2_rs, part.at[2])
    fin_v[0] = part[2, 0:4, :]
    fin_v[1] = part[2, 4:8, :]
    swap = remote(fin_v.at[1 - c], fin_v.at[2], s_ss.at[4], s_rs.at[4], sib)
    swap.start()

    def own(v):
        return jnp.where(c == 0, v[0:4, :], v[4:8, :])
    out_ref[:, pl.ds(mine, COLS)] = (own(part[0]) + fin_v[c]).astype(bf)
    swap.wait()
    out_ref[:, pl.ds(other, COLS)] = (own(part[1]) + fin_v[2]).astype(bf)

    @pl.loop(1, 64)
    def _(i):
        k, to = peer(i)
        remote(o_ref.at[k], x_v.at[k], a_ss.at[i], a_rs.at[k], to).wait_send()
    for cp in early:
        cp.wait_send()
    gather.drain()


def layer_call(lengths, qt, new, kt, ids, scores, residual, gain, uv, wo, wg, wu, wd):
    vm = pl.BlockSpec(memory_space=pltpu.VMEM)
    hbm = pl.BlockSpec(memory_space=pl.ANY)
    dma = pltpu.SemaphoreType.DMA
    return pl.pallas_call(
        layer_kernel, out_shape=jax.ShapeDtypeStruct((4, 2 * COLS), bf),
        in_specs=[pl.BlockSpec(memory_space=pltpu.SMEM), vm, vm, hbm, vm, vm, vm, vm, hbm, hbm, hbm, hbm, hbm], out_specs=vm,
        scratch_shapes=[
            pltpu.VMEM((512, KROWS), bf), pltpu.VMEM((128, 576), bf), pltpu.VMEM((8192 // T, KROWS, T), bf), pltpu.VMEM((512, T), f32), pltpu.VMEM((512, T), f32),
            pltpu.VMEM((512, 128), f32), pltpu.VMEM((512, 128), f32), pltpu.VMEM((512, 512), f32), pltpu.VMEM((64, 8, 512), bf),
            pltpu.VMEM((64, 8, 512), bf), pltpu.VMEM((512, 256), bf), pltpu.VMEM((256, COLS), bf), pltpu.VMEM((2, 2, COLS, 256), bf),
            pltpu.VMEM((512, COLS), bf), pltpu.VMEM((512, 256), bf), pltpu.VMEM((2, 512, 256), bf),
            pltpu.VMEM((4, 4, 4, 8, COLS), bf), pltpu.VMEM((4, 4, 4, 8, COLS), bf), pltpu.VMEM((3, 4, 8, COLS), bf), pltpu.VMEM((3, 8, COLS), bf),
            pltpu.VMEM((3, 8, COLS), f32), pltpu.VMEM((2, 4, 2 * COLS), bf), pltpu.VMEM((2, 4, 128), f32), pltpu.VMEM((4, 4, 4, 8, GCOLS), bf),
            pltpu.VMEM((2, 2, 512, 256), f32), pltpu.VMEM((2, 512, 256), bf), pltpu.VMEM((2, 512, 256), bf), pltpu.VMEM((512, 512), bf), pltpu.VMEM((3, 4, COLS), f32),
            dma((8192 // T,)), dma((64,)), dma((64,)), dma((7,)), dma((7,)), dma((7,)), dma((5,)), dma((5,)),
            *[dma((GROUPS, 3, 10)) for _ in range(6)]],
        compiler_params=pltpu.CompilerParams(collective_id=1, has_side_effects=True, vmem_limit_bytes=60 << 20),
    )(lengths, qt, new, kt, ids, scores, residual, gain, uv, wo, wg, wu, wd)


def per_device(queries, new_latent, cache_latent, cache_len, route_ids, route_scores, residual, norm_gain,
               w_uv, w_out, w_gate, w_up, w_down):
    return layer_call(cache_len[None], jnp.swapaxes(queries[0], 1, 2), new_latent[0], jnp.swapaxes(cache_latent[0], 0, 1), route_ids[0], route_scores[0],
                      residual[0], norm_gain[None], w_uv[0], w_out[0], w_gate[0], w_up[0], w_down[0])[None]


def solution(mesh):
    r = ("sec", "ep")
    placed = (P(r, None, None, None), P(r, None, None), P(r, None, None), P(r), P(r, None, None), P(r, None, None), P(r, None, None),
              P(), P(r, None, None), P(r, None, None), P("ep", None, "sec"), P("ep", None, "sec"), P("ep", "sec", None))
    return jax.shard_map(per_device, mesh=mesh, in_specs=placed, out_specs=P(r, None, None), check_vma=False)
```

```python
import functools
import jax, jax.numpy as jnp
from jax import lax
from jax.experimental import pallas as pl
from jax.experimental.pallas import tpu as pltpu
from jax.sharding import PartitionSpec as P

MESH = pl.DeviceIdType.MESH
f32 = jnp.float32
bf = jnp.bfloat16
COLS = 3584
GCOLS = 3712
ORDERS = ((0, 1, 2), (1, 2, 0), (2, 0, 1))


def streams(groups):
    start, made = 0, []
    for tiles, halves in groups:
        made.append([])
        for p in range(3):
            made[-1].append((start, tiles[p] * 128, halves[p] * 128, ORDERS[p]))
            start += tiles[p] * 128
    return made


RS = streams((((5, 5, 4), (3, 3, 2)), ((5, 4, 5), (2, 2, 2))))
AG = streams((((5, 5, 4), (3, 3, 2)), ((5, 5, 5), (2, 2, 3))))
GROUPS = len(RS)
WIDTH = COLS // GROUPS


def dev(pos, c):
    return (pos[0], (pos[1] * 4 + pos[2]) * 2 + c)


def shifted(pos, axis, by):
    out = list(pos)
    out[axis] = (pos[axis] + by) % 4
    return tuple(out)


def remote(src, dst, ss, rs, to):
    return pltpu.make_async_remote_copy(src_ref=src, dst_ref=dst, send_sem=ss, recv_sem=rs, device_id=to, device_id_type=MESH)


def region(pos, stream, stage, q, lo=0, hi=None):
    start, width, _, order = stream
    idx = [slice(None)] * 3
    for k in range(stage):
        idx[order[k]] = pos[order[k]]
    idx[order[stage]] = q
    return tuple(idx) + (slice(None), slice(start + lo, start + (width if hi is None else hi)))


def halves(stream):
    _, width, half, _ = stream
    return ((0, 1, 0, half), (1, 3, half, width))


class ReduceScatter:
    def __init__(self, pos, c, acc, bufs, ss, rs, out):
        self.pos, self.c, self.acc, self.bufs, self.ss, self.rs, self.out = pos, c, acc, bufs, ss, rs, out
        self.copies = {}

    def reg(self, st, stage, q, lo=0, hi=None):
        return self.acc.at[region(self.pos, st, stage, q, lo, hi)]

    def slot(self, st, stage, d, lo=0, hi=None):
        start, width = st[:2]
        return self.bufs[stage].at[(d,) + (slice(None),) * (2 - stage) + (slice(None), slice(start + lo, start + (width if hi is None else hi)))]

    def send(self, g, p, n, src, dst, axis, by):
        cp = remote(src, dst, self.ss.at[g, p, n], self.rs.at[g, p, n], dev(shifted(self.pos, axis, by), self.c))
        cp.start()
        self.copies[g, p, n] = cp

    def total(self, g, p, st, stage, first, count):
        axis = st[3][stage]
        total = self.reg(st, stage, self.pos[axis])[...].astype(f32)
        for d in range(count):
            self.copies[g, p, first + d].wait_recv()
            total += self.slot(st, stage, d)[...].astype(f32)
        return total

    def step(self, g, k):
        pos = self.pos
        for p, st in enumerate(RS[g]):
            start, width, _, order = st
            if k == 0:
                for d, by, lo, hi in halves(st):
                    self.send(g, p, d, self.reg(st, 0, (pos[order[0]] + 2) % 4, lo, hi), self.slot(st, 0, 2 + d, lo, hi), order[0], by)
            elif k == 1:
                for d, by, lo, hi in halves(st):
                    q = (pos[order[0]] + by) % 4
                    self.copies[g, p, d].wait_recv()
                    dst = self.reg(st, 0, q, lo, hi)
                    dst[...] = (dst[...].astype(f32) + self.slot(st, 0, 2 + d, lo, hi)[...].astype(f32)).astype(bf)
                for d, by in ((0, 1), (1, 3)):
                    q = (pos[order[0]] + by) % 4
                    self.send(g, p, 2 + d, self.reg(st, 0, q), self.slot(st, 0, d), order[0], by)
            elif k in (2, 3):
                stage = k - 1
                mine = self.reg(st, stage - 1, pos[order[stage - 1]])
                mine[...] = (self.total(g, p, st, 0, 2, 2) if k == 2 else self.total(g, p, st, 1, 4, 3)).astype(bf)
                for by in (1, 2, 3):
                    q = (pos[order[stage]] + by) % 4
                    self.send(g, p, 1 + 3 * stage + by - 1, self.reg(st, stage, q), self.slot(st, stage, by - 1), order[stage], by)
            else:
                self.out[:, start:start + width] = self.total(g, p, st, 2, 7, 3)

    def drain(self):
        for cp in self.copies.values():
            cp.wait_send()


class AllGather:
    def __init__(self, pos, c, g, ss, rs):
        self.pos, self.c, self.g, self.ss, self.rs = pos, c, g, ss, rs
        self.copies = {}

    def send(self, g, p, n, st, stage, q, lo, hi, axis, by):
        r = self.g.at[region(self.pos, st, stage, q, lo, hi)]
        cp = remote(r, r, self.ss.at[g, p, n], self.rs.at[g, p, n], dev(shifted(self.pos, axis, by), self.c))
        cp.start()
        self.copies[g, p, n] = cp

    def arrived(self, g, p, *which):
        for n in which:
            self.copies[g, p, n].wait_recv()

    def step(self, g, k):
        pos = self.pos
        for p, st in enumerate(AG[g]):
            order = st[3]
            if k in (0, 1):
                stage = 2 - k
                if k == 1:
                    self.arrived(g, p, 7, 8, 9)
                for by in (1, 2, 3):
                    self.send(g, p, 1 + 3 * stage + by - 1, st, stage, pos[order[stage]], 0, None, order[stage], by)
            elif k == 2:
                self.arrived(g, p, 4, 5, 6)
                for d, by in ((0, 1), (1, 3)):
                    self.send(g, p, d, st, 0, pos[order[0]], 0, None, order[0], by)
            elif k == 3:
                for d, by, lo, hi in halves(st):
                    self.arrived(g, p, d)
                    self.send(g, p, 2 + d, st, 0, (pos[order[0]] + 4 - by) % 4, lo, hi, order[0], by)
            else:
                self.arrived(g, p, 2, 3)

    def drain(self):
        for cp in self.copies.values():
            cp.wait_send()


T = 1024
KROWS = 592
SCORE = (192.0 ** -0.5) * 1.4426950408889634


def attention(len_ref, qt_ref, new_ref, kt_ref, q_sc, n_sc, kbuf, s_a, s_b, m_sc, l_sc, acc_sc, k_sem, between):
    blocks = kbuf.shape[0]
    copies = [pltpu.make_async_copy(kt_ref.at[:, i * T:(i + 1) * T], kbuf.at[i, 0:576, :], k_sem.at[i]) for i in range(blocks)]
    for cp in copies:
        cp.start()
    n = len_ref[0, 0]
    edge = lax.broadcasted_iota(jnp.int32, (16, T), 0)
    lane = lax.broadcasted_iota(jnp.int32, (16, T), 1)
    for i in range(blocks):
        kbuf[i, 576:592, :] = jnp.where((edge == 0) & (lane + i * T >= n), -1e30, 0.0).astype(bf)
    r0 = lax.broadcasted_iota(jnp.int32, (512, 512), 0)
    r1 = lax.broadcasted_iota(jnp.int32, (512, 512), 1)
    order = jnp.where((r0 % 4) * 128 + r0 // 4 == r1, 1.0, 0.0).astype(bf)
    q = jnp.concatenate([qt_ref[s].T for s in range(4)], axis=0)
    q_sc[:, 0:576] = jnp.dot(order, q, preferred_element_type=f32).astype(bf)
    q_sc[:, 576:592] = jnp.where(lax.broadcasted_iota(jnp.int32, (512, 16), 1) == 0, 1.0, 0.0).astype(bf)
    n_sc[...] = jnp.zeros_like(n_sc)
    n_sc[0:4, :] = new_ref[...]
    s = lax.dot_general(q_sc[:, 0:576], n_sc[...], (((1,), (1,)), ((), ())), preferred_element_type=f32) * SCORE
    row = lax.broadcasted_iota(jnp.int32, s.shape, 0)
    col = lax.broadcasted_iota(jnp.int32, s.shape, 1)
    s = jnp.where(col <= row % 4, s, -1e30)
    m = jnp.max(s, axis=1, keepdims=True)
    p = jnp.exp2(s - m)
    m_sc[...] = jnp.broadcast_to(m, (512, 128))
    l_sc[...] = jnp.broadcast_to(jnp.sum(p, axis=1, keepdims=True), (512, 128))
    acc_sc[...] = jnp.dot(p.astype(bf), n_sc[:, 0:512], preferred_element_type=f32)

    def scores(i, into):
        into[...] = jnp.dot(q_sc[...], kbuf[i], preferred_element_type=f32)

    def fold(i, s_ref):
        s = s_ref[...]
        old = m_sc[...]
        new = jnp.maximum(old, jnp.max(s, axis=1, keepdims=True) * SCORE)
        shrink = jnp.exp2(old - new)
        p = jnp.exp2(s * SCORE - new[:, 0:1])
        l_sc[...] = l_sc[...] * shrink + jnp.sum(p, axis=1, keepdims=True)
        m_sc[...] = new
        pv = lax.dot_general(p.astype(bf), kbuf[i, 0:512, :], (((1,), (1,)), ((), ())), preferred_element_type=f32)
        acc_sc[...] = acc_sc[...] * shrink[:, 0:1] + pv

    copies[0].wait()
    scores(0, s_a)
    for i in range(blocks):
        if i + 1 < blocks:
            copies[i + 1].wait()
            scores(i + 1, (s_a, s_b)[(i + 1) % 2])
        fold(i, (s_a, s_b)[i % 2])
        if i in between:
            between[i]()
    return acc_sc[...] * (1.0 / l_sc[:, 0:1])


def layer_kernel(len_ref, qt_ref, new_ref, kt_ref, ids_ref, sc_ref, res_ref, gain_ref, uv_hbm, wo_hbm, wg_hbm, wu_hbm, wd_hbm, out_ref,
                 q_sc, n_sc, kbuf, s_a, s_b, m_sc, l_sc, acc_sc, o_ref, x_v, uv_v, wo_v, w_v, wd_v, h_v, hs_v, acc, b0, b1, b2, part, res_v, cf_v, g_v, gu_v, snd_v, rcv_v, act_v, fin_v,
                 k_sem, t_sem, a_ss, a_rs, l_sem, w_ss, w_rs, s_ss, s_rs, r1_ss, r1_rs, g_ss, g_rs, r2_ss, r2_rs):
    z = lax.axis_index("sec")
    e = lax.axis_index("ep")
    x, y, c = e // 8, (e // 2) % 4, e % 2
    pos = (z, x, y)
    me = z * 16 + x * 4 + y
    sib = dev(pos, 1 - c)
    mine = pl.multiple_of(c * COLS, 128)
    other = pl.multiple_of((1 - c) * COLS, 128)

    def peer(i):
        k = (me + i) % 64
        return k, (k // 16, (k % 16) * 2 + c)

    barrier = pltpu.get_barrier_semaphore()

    def tell(axis, sem):
        for by in (1, 2, 3):
            pl.semaphore_signal(sem, inc=1, device_id=dev(shifted(pos, axis, by), c), device_id_type=MESH)

    for axis in range(3):
        tell(axis, barrier)
    pl.semaphore_signal(barrier, inc=1, device_id=sib, device_id_type=MESH)

    uvc = pl.ds(pl.multiple_of(c * 128, 128), 128)
    local = [pltpu.make_async_copy(a, b, l_sem.at[i]) for i, (a, b) in enumerate((
        (o_ref.at[me], x_v.at[me]),
        (uv_hbm, uv_v.at[:, uvc]),
        (wo_hbm.at[:, pl.ds(mine, COLS)], wo_v.at[pl.ds(pl.multiple_of(c * 128, 128), 128), :]),
        (wg_hbm.at[pl.ds(mine, COLS), :], w_v.at[c, 0]),
        (wu_hbm.at[pl.ds(mine, COLS), :], w_v.at[c, 1]),
        (wd_hbm.at[:, pl.ds(mine, COLS)], wd_v.at[pl.ds(pl.multiple_of(c * 256, 256), 256), :]),
        (res_ref, res_v.at[c]),
    ))]
    for i in (1, 2, 6):
        local[i].start()
    sc = sc_ref[...]
    shares = sc / jnp.sum(sc, axis=1, keepdims=True) * 2.5
    ids = ids_ref[...]
    lane = lax.broadcasted_iota(jnp.int32, (4, 128), 1)
    coef = jnp.zeros((4, 128), f32)
    for k in range(8):
        coef += jnp.where(lane % 32 == ids[:, k:k + 1], shares[:, k:k + 1], 0.0)
    high = coef.astype(bf).astype(f32)
    cf_v[c] = jnp.where(lane < 32, high, jnp.where(lane < 64, coef - high, 0.0))

    early = [remote(a, b, w_ss.at[i], w_rs.at[i], sib) for i, (a, b) in enumerate((
        (uv_hbm, uv_v.at[:, uvc]),
        (wo_hbm.at[:, pl.ds(other, COLS)], wo_v.at[pl.ds(pl.multiple_of(c * 128, 128), 128), :]),
        (wg_hbm.at[pl.ds(other, COLS), :], w_v.at[c, 0]),
        (wu_hbm.at[pl.ds(other, COLS), :], w_v.at[c, 1]),
        (wd_hbm.at[:, pl.ds(other, COLS)], wd_v.at[pl.ds(pl.multiple_of(c * 256, 256), 256), :]),
        (res_ref, res_v.at[c]),
        (cf_v.at[c], cf_v.at[c]),
    ))]
    def exchange_weights():
        pl.semaphore_wait(barrier, 10)
        tell(1, t_sem.at[0])
        for i in (0, 1, 5, 6, 2, 3, 4):
            early[i].start()
        for cp in local[3:6]:
            cp.start()

    def second_turn():
        pl.semaphore_wait(t_sem.at[0], 3)
        tell(2, t_sem.at[1])

    latent = attention(len_ref, qt_ref, new_ref, kt_ref, q_sc, n_sc, kbuf, s_a, s_b, m_sc, l_sc, acc_sc, k_sem, {1: exchange_weights, 4: second_turn})
    pl.semaphore_wait(t_sem.at[1], 3)
    o_ref.reshape(512, 512)[...] = latent.astype(bf)
    local[0].start()

    @pl.loop(1, 64, unroll=7)
    def _(i):
        k, to = peer(i)
        remote(o_ref.at[k], x_v.at[me], a_ss, a_rs, to).start()

    for i in (0, 1, 2):
        local[i].wait()
    for i in (0, 1):
        early[i].wait_recv()

    latents = remote(o_ref.at[pl.ds(0, 63)], x_v.at[pl.ds(0, 63)], a_ss, a_rs, sib)
    latents.wait_recv()

    m = jnp.dot(x_v.reshape(512, 512)[...], uv_v[...], preferred_element_type=f32)
    row = lax.broadcasted_iota(jnp.int32, (512, 256), 0)
    col = lax.broadcasted_iota(jnp.int32, (512, 256), 1)
    m = jnp.where((row // 4) % 2 == col // 128, m, 0.0).astype(bf)
    t = lax.broadcasted_iota(jnp.int32, (512, 512), 0)
    r = lax.broadcasted_iota(jnp.int32, (512, 512), 1)
    put = jnp.where((t // 8 == r // 8) & (t % 4 == r % 4) & ((t // 4) % 2 == c), 1.0, 0.0).astype(bf)
    hs_v[0] = jnp.dot(put, m, preferred_element_type=f32).astype(bf)
    swap = remote(hs_v.at[0], hs_v.at[1], s_ss.at[0], s_rs.at[0], sib)
    swap.start()
    swap.wait()
    h_v[...] = hs_v[0] + hs_v[1]
    acc2 = acc.reshape(512, COLS)

    def project(a, w, g):
        for half in range(2):
            cols = slice(g * WIDTH + half * (WIDTH // 2), g * WIDTH + (half + 1) * (WIDTH // 2))
            acc2[:, cols] = jnp.dot(a[...], w[:, cols], preferred_element_type=f32).astype(bf)

    def project_and_reduce(a, w, ss, rs, out, aside):
        sums = ReduceScatter(pos, c, acc, (b0, b1, b2), ss, rs, out)
        for k in range(5):
            for g in range(GROUPS):
                if k == 0:
                    project(a, w, g)
                sums.step(g, k)
            if k == 0:
                aside()
        return sums

    def sent_latents():
        latents.wait_send()
        for i in (0, 1):
            early[i].wait_send()

    sums = project_and_reduce(h_v, wo_v, r1_ss, r1_rs, part.at[0], sent_latents)
    swap = remote(part.at[0], part.at[1], s_ss.at[1], s_rs.at[1], sib)
    swap.start()
    sums.drain()
    local[6].wait()
    early[5].wait_recv()
    early[6].wait_recv()
    res8 = lambda cols: jnp.concatenate([res_v[0, :, cols].astype(f32), res_v[1, :, cols].astype(f32)], axis=0)
    swap.wait()
    part[0] += res8(pl.ds(mine, COLS))
    part[1] += res8(pl.ds(other, COLS))
    squares = jnp.sum(part[0] * part[0], axis=1, keepdims=True) + jnp.sum(part[1] * part[1], axis=1, keepdims=True)
    scale = lax.rsqrt(squares * (1.0 / (2 * COLS)) + 1e-06)
    gmine = g_v.at[z, x, y]
    gain = jnp.where(c == 0, gain_ref[0:28, :].astype(f32), gain_ref[28:56, :].astype(f32))
    gain = jnp.concatenate([gain[i:i + 1, :] for i in range(28)], axis=1)
    gmine[:, :COLS] = (part[0] * scale * gain).astype(bf)
    gmine[:, COLS:] = jnp.concatenate([cf_v[0], cf_v[1]], axis=0).astype(bf)

    gather = AllGather(pos, c, g_v, g_ss, g_rs)
    tokens = g_v.reshape(512, GCOLS)
    for k in range(4):
        for g in range(GROUPS):
            gather.step(g, k)
    for i in (3, 4):
        local[i].wait()
    for i in (2, 3):
        early[i].wait_recv()

    def product(which, gu, g):
        rows = slice(g * WIDTH, (g + 1) * WIDTH)
        return jnp.dot(tokens[:, rows], w_v[which, gu, rows, :], preferred_element_type=f32)

    for g in range(GROUPS):
        gather.step(g, 4)
        for n, which in ((0, 1 - c), (1, c)):
            for gu in (0, 1):
                new = product(which, gu, g)
                if g > 0:
                    new += gu_v[n, gu]
                if g < GROUPS - 1:
                    gu_v[n, gu] = new
                elif n == 0:
                    snd_v[gu] = new.astype(bf)
                else:
                    gu_v[n, gu] = new
            if n == 0 and g == GROUPS - 1:
                swap = remote(snd_v, rcv_v, s_ss.at[2], s_rs.at[2], sib)
                swap.start()
    coefs = tokens[:, COLS:].astype(f32)
    lane = lax.broadcasted_iota(jnp.int32, (512, 128), 1)
    column = jnp.sum(jnp.where((lane % 32 == e) & (lane < 64), coefs, 0.0), axis=1, keepdims=True)
    swap.wait()
    gate = gu_v[1, 0] + rcv_v[0].astype(f32)
    up = gu_v[1, 1] + rcv_v[1].astype(f32)
    acts = act_v.at[:, pl.ds(pl.multiple_of(c * 256, 256), 256)]
    acts[...] = (gate / (1.0 + jnp.exp(-gate)) * up * column).astype(bf)
    swap = remote(acts, acts, s_ss.at[3], s_rs.at[3], sib)
    swap.start()
    local[5].wait()
    early[4].wait_recv()
    swap.wait()
    def sent_tokens():
        for i in range(2, 7):
            early[i].wait_send()
        gather.drain()

    sums = project_and_reduce(act_v, wd_v, r2_ss, r2_rs, part.at[2], sent_tokens)
    fin_v[0] = part[2, 0:4, :]
    fin_v[1] = part[2, 4:8, :]
    swap = remote(fin_v.at[1 - c], fin_v.at[2], s_ss.at[4], s_rs.at[4], sib)
    swap.start()

    def own(v):
        return jnp.where(c == 0, v[0:4, :], v[4:8, :])
    out_ref[:, pl.ds(mine, COLS)] = (own(part[0]) + fin_v[c]).astype(bf)
    sums.drain()
    swap.wait()
    out_ref[:, pl.ds(other, COLS)] = (own(part[1]) + fin_v[2]).astype(bf)


def layer_call(lengths, qt, new, kt, ids, scores, residual, gain, uv, wo, wg, wu, wd):
    vm = pl.BlockSpec(memory_space=pltpu.VMEM)
    hbm = pl.BlockSpec(memory_space=pl.ANY)
    dma = pltpu.SemaphoreType.DMA
    return pl.pallas_call(
        layer_kernel, out_shape=jax.ShapeDtypeStruct((4, 2 * COLS), bf),
        in_specs=[pl.BlockSpec(memory_space=pltpu.SMEM), vm, vm, hbm, vm, vm, vm, vm, hbm, hbm, hbm, hbm, hbm], out_specs=vm,
        scratch_shapes=[
            pltpu.VMEM((512, KROWS), bf), pltpu.VMEM((128, 576), bf), pltpu.VMEM((8192 // T, KROWS, T), bf), pltpu.VMEM((512, T), f32), pltpu.VMEM((512, T), f32),
            pltpu.VMEM((512, 128), f32), pltpu.VMEM((512, 128), f32), pltpu.VMEM((512, 512), f32), pltpu.VMEM((64, 8, 512), bf),
            pltpu.VMEM((64, 8, 512), bf), pltpu.VMEM((512, 256), bf), pltpu.VMEM((256, COLS), bf), pltpu.VMEM((2, 2, COLS, 256), bf),
            pltpu.VMEM((512, COLS), bf), pltpu.VMEM((512, 256), bf), pltpu.VMEM((2, 512, 256), bf),
            pltpu.VMEM((4, 4, 4, 8, COLS), bf), pltpu.VMEM((4, 4, 4, 8, COLS), bf), pltpu.VMEM((3, 4, 8, COLS), bf), pltpu.VMEM((3, 8, COLS), bf),
            pltpu.VMEM((3, 8, COLS), f32), pltpu.VMEM((2, 4, 2 * COLS), bf), pltpu.VMEM((2, 4, 128), f32), pltpu.VMEM((4, 4, 4, 8, GCOLS), bf),
            pltpu.VMEM((2, 2, 512, 256), f32), pltpu.VMEM((2, 512, 256), bf), pltpu.VMEM((2, 512, 256), bf), pltpu.VMEM((512, 512), bf), pltpu.VMEM((3, 4, COLS), f32),
            dma((8192 // T,)), pltpu.SemaphoreType.REGULAR((2,)), dma, dma, dma((7,)), dma((7,)), dma((7,)), dma((5,)), dma((5,)),
            *[dma((GROUPS, 3, 10)) for _ in range(6)]],
        compiler_params=pltpu.CompilerParams(collective_id=1, has_side_effects=True, vmem_limit_bytes=60 << 20),
    )(lengths, qt, new, kt, ids, scores, residual, gain, uv, wo, wg, wu, wd)


def per_device(queries, new_latent, cache_latent, cache_len, route_ids, route_scores, residual, norm_gain,
               w_uv, w_out, w_gate, w_up, w_down):
    return layer_call(cache_len[None], jnp.swapaxes(queries[0], 1, 2), new_latent[0], jnp.swapaxes(cache_latent[0], 0, 1), route_ids[0], route_scores[0],
                      residual[0], norm_gain.reshape(56, 128), w_uv[0], w_out[0], w_gate[0], w_up[0], w_down[0])[None]


def solution(mesh):
    r = ("sec", "ep")
    placed = (P(r, None, None, None), P(r, None, None), P(r, None, None), P(r), P(r, None, None), P(r, None, None), P(r, None, None),
              P(), P(r, None, None), P(r, None, None), P("ep", None, "sec"), P("ep", None, "sec"), P("ep", "sec", None))
    return jax.shard_map(per_device, mesh=mesh, in_specs=placed, out_specs=P(r, None, None), check_vma=False)
```

```python
import functools
import jax, jax.numpy as jnp
from jax import lax
from jax.experimental import pallas as pl
from jax.experimental.pallas import tpu as pltpu
from jax.sharding import PartitionSpec as P

MESH = pl.DeviceIdType.MESH
f32 = jnp.float32
bf = jnp.bfloat16
COLS = 3584
GCOLS = 3712
ORDERS = ((0, 1, 2), (1, 2, 0), (2, 0, 1))


def streams(groups):
    start, made = 0, []
    for tiles, halves in groups:
        made.append([])
        for p in range(3):
            made[-1].append((start, tiles[p] * 128, halves[p] * 128, ORDERS[p]))
            start += tiles[p] * 128
    return made


RS = streams((((5, 5, 4), (3, 3, 2)), ((5, 4, 5), (2, 2, 2))))
AG = streams((((5, 5, 4), (3, 3, 2)), ((5, 5, 5), (2, 2, 3))))
GROUPS = len(RS)
WIDTH = COLS // GROUPS


def dev(pos, c):
    return (pos[0], (pos[1] * 4 + pos[2]) * 2 + c)


def shifted(pos, axis, by):
    out = list(pos)
    out[axis] = (pos[axis] + by) % 4
    return tuple(out)


def remote(src, dst, ss, rs, to):
    return pltpu.make_async_remote_copy(src_ref=src, dst_ref=dst, send_sem=ss, recv_sem=rs, device_id=to, device_id_type=MESH)


def region(pos, stream, stage, q, lo=0, hi=None):
    start, width, _, order = stream
    idx = [slice(None)] * 3
    for k in range(stage):
        idx[order[k]] = pos[order[k]]
    idx[order[stage]] = q
    return tuple(idx) + (slice(None), slice(start + lo, start + (width if hi is None else hi)))


def halves(stream):
    _, width, half, _ = stream
    return ((0, 1, 0, half), (1, 3, half, width))


def rests(stream):
    _, width, half, _ = stream
    return ((0, 1, half, width), (1, 3, 0, half))


class ReduceScatter:
    def __init__(self, pos, c, acc, bufs, ss, rs, out):
        self.pos, self.c, self.acc, self.bufs, self.ss, self.rs, self.out = pos, c, acc, bufs, ss, rs, out
        self.copies = {}

    def reg(self, st, stage, q, lo=0, hi=None):
        return self.acc.at[region(self.pos, st, stage, q, lo, hi)]

    def slot(self, st, stage, d, lo=0, hi=None):
        start, width = st[:2]
        return self.bufs[stage].at[(d,) + (slice(None),) * (2 - stage) + (slice(None), slice(start + lo, start + (width if hi is None else hi)))]

    def send(self, g, p, n, src, dst, axis, by):
        cp = remote(src, dst, self.ss.at[g, p, n], self.rs.at[g, p, n], dev(shifted(self.pos, axis, by), self.c))
        cp.start()
        self.copies[g, p, n] = cp

    def total(self, g, p, st, stage, first, count):
        axis = st[3][stage]
        total = self.reg(st, stage, self.pos[axis])[...].astype(f32)
        for d in range(count):
            self.copies[g, p, first + d].wait_recv()
            if stage == 0:
                self.copies[g, p, 10 + d].wait_recv()
            total += self.slot(st, stage, d)[...].astype(f32)
        return total

    def step(self, g, k):
        pos = self.pos
        for p, st in enumerate(RS[g]):
            start, width, _, order = st
            if k == 0:
                for d, by, lo, hi in halves(st):
                    self.send(g, p, d, self.reg(st, 0, (pos[order[0]] + 2) % 4, lo, hi), self.slot(st, 0, 2 + d, lo, hi), order[0], by)
            elif k == 1:
                for d, by, lo, hi in halves(st):
                    q = (pos[order[0]] + by) % 4
                    self.copies[g, p, d].wait_recv()
                    dst = self.reg(st, 0, q, lo, hi)
                    dst[...] = (dst[...].astype(f32) + self.slot(st, 0, 2 + d, lo, hi)[...].astype(f32)).astype(bf)
                    self.send(g, p, 2 + d, self.reg(st, 0, q, lo, hi), self.slot(st, 0, d, lo, hi), order[0], by)
            elif k in (2, 3):
                stage = k - 1
                mine = self.reg(st, stage - 1, pos[order[stage - 1]])
                mine[...] = (self.total(g, p, st, 0, 2, 2) if k == 2 else self.total(g, p, st, 1, 4, 3)).astype(bf)
                for by in (1, 2, 3):
                    q = (pos[order[stage]] + by) % 4
                    self.send(g, p, 1 + 3 * stage + by - 1, self.reg(st, stage, q), self.slot(st, stage, by - 1), order[stage], by)
            else:
                self.out[:, start:start + width] = self.total(g, p, st, 2, 7, 3)
        if k == 0:
            for p, st in enumerate(RS[g]):
                axis = st[3][0]
                for d, by, lo, hi in rests(st):
                    self.send(g, p, 10 + d, self.reg(st, 0, (pos[axis] + by) % 4, lo, hi), self.slot(st, 0, d, lo, hi), axis, by)

    def drain(self):
        for cp in self.copies.values():
            cp.wait_send()


class AllGather:
    def __init__(self, pos, c, g, ss, rs):
        self.pos, self.c, self.g, self.ss, self.rs = pos, c, g, ss, rs
        self.copies = {}

    def send(self, g, p, n, st, stage, q, lo, hi, axis, by):
        r = self.g.at[region(self.pos, st, stage, q, lo, hi)]
        cp = remote(r, r, self.ss.at[g, p, n], self.rs.at[g, p, n], dev(shifted(self.pos, axis, by), self.c))
        cp.start()
        self.copies[g, p, n] = cp

    def arrived(self, g, p, *which):
        for n in which:
            self.copies[g, p, n].wait_recv()

    def step(self, g, k):
        pos = self.pos
        for p, st in enumerate(AG[g]):
            order = st[3]
            if k in (0, 1):
                stage = 2 - k
                if k == 1:
                    self.arrived(g, p, 7, 8, 9)
                for by in (1, 2, 3):
                    self.send(g, p, 1 + 3 * stage + by - 1, st, stage, pos[order[stage]], 0, None, order[stage], by)
            elif k == 2:
                self.arrived(g, p, 4, 5, 6)
                for d, by, lo, hi in halves(st):
                    self.send(g, p, d, st, 0, pos[order[0]], lo, hi, order[0], by)
                for d, by, lo, hi in rests(st):
                    self.send(g, p, 10 + d, st, 0, pos[order[0]], lo, hi, order[0], by)
            elif k == 3:
                for d, by, lo, hi in halves(st):
                    self.arrived(g, p, d)
                    self.send(g, p, 2 + d, st, 0, (pos[order[0]] + 4 - by) % 4, lo, hi, order[0], by)
            else:
                self.arrived(g, p, 2, 3, 10, 11)

    def drain(self):
        for cp in self.copies.values():
            cp.wait_send()


T = 1024
KROWS = 592
SCORE = (192.0 ** -0.5) * 1.4426950408889634


def attention(len_ref, qt_ref, new_ref, kt_ref, q_sc, n_sc, kbuf, s_a, s_b, m_sc, l_sc, acc_sc, k_sem, between):
    blocks = kbuf.shape[0]
    copies = [pltpu.make_async_copy(kt_ref.at[:, i * T:(i + 1) * T], kbuf.at[i, 0:576, :], k_sem.at[i]) for i in range(blocks)]
    for cp in copies:
        cp.start()
    n = len_ref[0, 0]
    edge = lax.broadcasted_iota(jnp.int32, (16, T), 0)
    lane = lax.broadcasted_iota(jnp.int32, (16, T), 1)
    for i in range(blocks):
        kbuf[i, 576:592, :] = jnp.where((edge == 0) & (lane + i * T >= n), -1e30, 0.0).astype(bf)
    r0 = lax.broadcasted_iota(jnp.int32, (512, 512), 0)
    r1 = lax.broadcasted_iota(jnp.int32, (512, 512), 1)
    order = jnp.where((r0 % 4) * 128 + r0 // 4 == r1, 1.0, 0.0).astype(bf)
    q = jnp.concatenate([qt_ref[s].T for s in range(4)], axis=0)
    q_sc[:, 0:576] = jnp.dot(order, q, preferred_element_type=f32).astype(bf)
    q_sc[:, 576:592] = jnp.where(lax.broadcasted_iota(jnp.int32, (512, 16), 1) == 0, 1.0, 0.0).astype(bf)
    n_sc[...] = jnp.zeros_like(n_sc)
    n_sc[0:4, :] = new_ref[...]
    s = lax.dot_general(q_sc[:, 0:576], n_sc[...], (((1,), (1,)), ((), ())), preferred_element_type=f32) * SCORE
    row = lax.broadcasted_iota(jnp.int32, s.shape, 0)
    col = lax.broadcasted_iota(jnp.int32, s.shape, 1)
    s = jnp.where(col <= row % 4, s, -1e30)
    m = jnp.max(s, axis=1, keepdims=True)
    p = jnp.exp2(s - m)
    m_sc[...] = jnp.broadcast_to(m, (512, 128))
    l_sc[...] = jnp.broadcast_to(jnp.sum(p, axis=1, keepdims=True), (512, 128))
    acc_sc[...] = jnp.dot(p.astype(bf), n_sc[:, 0:512], preferred_element_type=f32)

    def scores(i, into):
        into[...] = jnp.dot(q_sc[...], kbuf[i], preferred_element_type=f32)

    def fold(i, s_ref):
        s = s_ref[...]
        old = m_sc[...]
        new = jnp.maximum(old, jnp.max(s, axis=1, keepdims=True) * SCORE)
        shrink = jnp.exp2(old - new)
        p = jnp.exp2(s * SCORE - new[:, 0:1])
        l_sc[...] = l_sc[...] * shrink + jnp.sum(p, axis=1, keepdims=True)
        m_sc[...] = new
        pv = lax.dot_general(p.astype(bf), kbuf[i, 0:512, :], (((1,), (1,)), ((), ())), preferred_element_type=f32)
        acc_sc[...] = acc_sc[...] * shrink[:, 0:1] + pv

    copies[0].wait()
    scores(0, s_a)
    for i in range(blocks):
        if i + 1 < blocks:
            copies[i + 1].wait()
            scores(i + 1, (s_a, s_b)[(i + 1) % 2])
        fold(i, (s_a, s_b)[i % 2])
        if i in between:
            between[i]()
    return acc_sc[...] * (1.0 / l_sc[:, 0:1])


def layer_kernel(len_ref, qt_ref, new_ref, kt_ref, ids_ref, sc_ref, res_ref, gain_ref, uv_hbm, wo_hbm, wg_hbm, wu_hbm, wd_hbm, out_ref,
                 q_sc, n_sc, kbuf, s_a, s_b, m_sc, l_sc, acc_sc, o_ref, x_v, uv_v, wo_v, w_v, wd_v, h_v, hs_v, acc, b0, b1, b2, part, res_v, cf_v, g_v, gu_v, snd_v, rcv_v, act_v, fin_v,
                 k_sem, t_sem, a_ss, a_rs, l_sem, w_ss, w_rs, s_ss, s_rs, r1_ss, r1_rs, g_ss, g_rs, r2_ss, r2_rs):
    z = lax.axis_index("sec")
    e = lax.axis_index("ep")
    x, y, c = e // 8, (e // 2) % 4, e % 2
    pos = (z, x, y)
    me = z * 16 + x * 4 + y
    sib = dev(pos, 1 - c)
    mine = pl.multiple_of(c * COLS, 128)
    other = pl.multiple_of((1 - c) * COLS, 128)

    def peer(i):
        k = (me + i) % 64
        return k, (k // 16, (k % 16) * 2 + c)

    barrier = pltpu.get_barrier_semaphore()

    def tell(axis, sem):
        for by in (1, 2, 3):
            pl.semaphore_signal(sem, inc=1, device_id=dev(shifted(pos, axis, by), c), device_id_type=MESH)

    for axis in range(3):
        tell(axis, barrier)
    pl.semaphore_signal(barrier, inc=1, device_id=sib, device_id_type=MESH)

    uvc = pl.ds(pl.multiple_of(c * 128, 128), 128)
    local = [pltpu.make_async_copy(a, b, l_sem.at[i]) for i, (a, b) in enumerate((
        (o_ref.at[me], x_v.at[me]),
        (uv_hbm, uv_v.at[:, uvc]),
        (wo_hbm.at[:, pl.ds(mine, COLS)], wo_v.at[pl.ds(pl.multiple_of(c * 128, 128), 128), :]),
        (wg_hbm.at[pl.ds(mine, COLS), :], w_v.at[c, 0]),
        (wu_hbm.at[pl.ds(mine, COLS), :], w_v.at[c, 1]),
        (wd_hbm.at[:, pl.ds(mine, COLS)], wd_v.at[pl.ds(pl.multiple_of(c * 256, 256), 256), :]),
        (res_ref, res_v.at[c]),
    ))]
    for i in (1, 2, 6):
        local[i].start()
    sc = sc_ref[...]
    shares = sc / jnp.sum(sc, axis=1, keepdims=True) * 2.5
    ids = ids_ref[...]
    lane = lax.broadcasted_iota(jnp.int32, (4, 128), 1)
    coef = jnp.zeros((4, 128), f32)
    for k in range(8):
        coef += jnp.where(lane % 32 == ids[:, k:k + 1], shares[:, k:k + 1], 0.0)
    high = coef.astype(bf).astype(f32)
    cf_v[c] = jnp.where(lane < 32, high, jnp.where(lane < 64, coef - high, 0.0))

    early = [remote(a, b, w_ss.at[i], w_rs.at[i], sib) for i, (a, b) in enumerate((
        (uv_hbm, uv_v.at[:, uvc]),
        (wo_hbm.at[:, pl.ds(other, COLS)], wo_v.at[pl.ds(pl.multiple_of(c * 128, 128), 128), :]),
        (wg_hbm.at[pl.ds(other, COLS), :], w_v.at[c, 0]),
        (wu_hbm.at[pl.ds(other, COLS), :], w_v.at[c, 1]),
        (wd_hbm.at[:, pl.ds(other, COLS)], wd_v.at[pl.ds(pl.multiple_of(c * 256, 256), 256), :]),
        (res_ref, res_v.at[c]),
        (cf_v.at[c], cf_v.at[c]),
    ))]
    def exchange_weights():
        pl.semaphore_wait(barrier, 10)
        tell(1, t_sem.at[0])
        for i in (0, 1, 5, 6, 2, 3, 4):
            early[i].start()
        for cp in local[3:6]:
            cp.start()

    def second_turn():
        pl.semaphore_wait(t_sem.at[0], 3)
        tell(2, t_sem.at[1])

    latent = attention(len_ref, qt_ref, new_ref, kt_ref, q_sc, n_sc, kbuf, s_a, s_b, m_sc, l_sc, acc_sc, k_sem, {1: exchange_weights, 4: second_turn})
    pl.semaphore_wait(t_sem.at[1], 3)
    o_ref.reshape(512, 512)[...] = latent.astype(bf)
    local[0].start()

    @pl.loop(1, 64, unroll=7)
    def _(i):
        k, to = peer(i)
        remote(o_ref.at[k], x_v.at[me], a_ss, a_rs, to).start()

    for i in (0, 1, 2):
        local[i].wait()
    for i in (0, 1):
        early[i].wait_recv()

    latents = remote(o_ref.at[pl.ds(0, 63)], x_v.at[pl.ds(0, 63)], a_ss, a_rs, sib)
    latents.wait_recv()

    m = jnp.dot(x_v.reshape(512, 512)[...], uv_v[...], preferred_element_type=f32)
    row = lax.broadcasted_iota(jnp.int32, (512, 256), 0)
    col = lax.broadcasted_iota(jnp.int32, (512, 256), 1)
    m = jnp.where((row // 4) % 2 == col // 128, m, 0.0).astype(bf)
    t = lax.broadcasted_iota(jnp.int32, (512, 512), 0)
    r = lax.broadcasted_iota(jnp.int32, (512, 512), 1)
    put = jnp.where((t // 8 == r // 8) & (t % 4 == r % 4) & ((t // 4) % 2 == c), 1.0, 0.0).astype(bf)
    hs_v[0] = jnp.dot(put, m, preferred_element_type=f32).astype(bf)
    swap = remote(hs_v.at[0], hs_v.at[1], s_ss.at[0], s_rs.at[0], sib)
    swap.start()
    swap.wait()
    h_v[...] = hs_v[0] + hs_v[1]
    acc2 = acc.reshape(512, COLS)

    def project(a, w, g):
        for half in range(2):
            cols = slice(g * WIDTH + half * (WIDTH // 2), g * WIDTH + (half + 1) * (WIDTH // 2))
            acc2[:, cols] = jnp.dot(a[...], w[:, cols], preferred_element_type=f32).astype(bf)

    def project_and_reduce(a, w, ss, rs, out, aside):
        sums = ReduceScatter(pos, c, acc, (b0, b1, b2), ss, rs, out)
        for k in range(5):
            for g in range(GROUPS):
                if k == 0:
                    project(a, w, g)
                sums.step(g, k)
            if k == 0:
                aside()
        return sums

    def sent_latents():
        latents.wait_send()
        for i in (0, 1):
            early[i].wait_send()

    sums = project_and_reduce(h_v, wo_v, r1_ss, r1_rs, part.at[0], sent_latents)
    swap = remote(part.at[0], part.at[1], s_ss.at[1], s_rs.at[1], sib)
    swap.start()
    sums.drain()
    local[6].wait()
    early[5].wait_recv()
    early[6].wait_recv()
    res8 = lambda cols: jnp.concatenate([res_v[0, :, cols].astype(f32), res_v[1, :, cols].astype(f32)], axis=0)
    swap.wait()
    part[0] += res8(pl.ds(mine, COLS))
    part[1] += res8(pl.ds(other, COLS))
    squares = jnp.sum(part[0] * part[0], axis=1, keepdims=True) + jnp.sum(part[1] * part[1], axis=1, keepdims=True)
    scale = lax.rsqrt(squares * (1.0 / (2 * COLS)) + 1e-06)
    gmine = g_v.at[z, x, y]
    gain = jnp.where(c == 0, gain_ref[0:28, :].astype(f32), gain_ref[28:56, :].astype(f32))
    gain = jnp.concatenate([gain[i:i + 1, :] for i in range(28)], axis=1)
    gmine[:, :COLS] = (part[0] * scale * gain).astype(bf)
    gmine[:, COLS:] = jnp.concatenate([cf_v[0], cf_v[1]], axis=0).astype(bf)

    gather = AllGather(pos, c, g_v, g_ss, g_rs)
    tokens = g_v.reshape(512, GCOLS)
    for k in range(4):
        for g in range(GROUPS):
            gather.step(g, k)
    for i in (3, 4):
        local[i].wait()
    for i in (2, 3):
        early[i].wait_recv()

    def product(which, gu, g):
        rows = slice(g * WIDTH, (g + 1) * WIDTH)
        return jnp.dot(tokens[:, rows], w_v[which, gu, rows, :], preferred_element_type=f32)

    for g in range(GROUPS):
        gather.step(g, 4)
        for n, which in ((0, 1 - c), (1, c)):
            for gu in (0, 1):
                new = product(which, gu, g)
                if g > 0:
                    new += gu_v[n, gu]
                if g < GROUPS - 1:
                    gu_v[n, gu] = new
                elif n == 0:
                    snd_v[gu] = new.astype(bf)
                else:
                    gu_v[n, gu] = new
            if n == 0 and g == GROUPS - 1:
                swap = remote(snd_v, rcv_v, s_ss.at[2], s_rs.at[2], sib)
                swap.start()
    coefs = tokens[:, COLS:].astype(f32)
    lane = lax.broadcasted_iota(jnp.int32, (512, 128), 1)
    column = jnp.sum(jnp.where((lane % 32 == e) & (lane < 64), coefs, 0.0), axis=1, keepdims=True)
    swap.wait()
    gate = gu_v[1, 0] + rcv_v[0].astype(f32)
    up = gu_v[1, 1] + rcv_v[1].astype(f32)
    acts = act_v.at[:, pl.ds(pl.multiple_of(c * 256, 256), 256)]
    acts[...] = (gate / (1.0 + jnp.exp(-gate)) * up * column).astype(bf)
    swap = remote(acts, acts, s_ss.at[3], s_rs.at[3], sib)
    swap.start()
    local[5].wait()
    early[4].wait_recv()
    swap.wait()
    def sent_tokens():
        for i in range(2, 7):
            early[i].wait_send()
        gather.drain()

    sums = project_and_reduce(act_v, wd_v, r2_ss, r2_rs, part.at[2], sent_tokens)
    fin_v[0] = part[2, 0:4, :]
    fin_v[1] = part[2, 4:8, :]
    swap = remote(fin_v.at[1 - c], fin_v.at[2], s_ss.at[4], s_rs.at[4], sib)
    swap.start()

    def own(v):
        return jnp.where(c == 0, v[0:4, :], v[4:8, :])
    out_ref[:, pl.ds(mine, COLS)] = (own(part[0]) + fin_v[c]).astype(bf)
    sums.drain()
    swap.wait()
    out_ref[:, pl.ds(other, COLS)] = (own(part[1]) + fin_v[2]).astype(bf)


def layer_call(lengths, qt, new, kt, ids, scores, residual, gain, uv, wo, wg, wu, wd):
    vm = pl.BlockSpec(memory_space=pltpu.VMEM)
    hbm = pl.BlockSpec(memory_space=pl.ANY)
    dma = pltpu.SemaphoreType.DMA
    return pl.pallas_call(
        layer_kernel, out_shape=jax.ShapeDtypeStruct((4, 2 * COLS), bf),
        in_specs=[pl.BlockSpec(memory_space=pltpu.SMEM), vm, vm, hbm, vm, vm, vm, vm, hbm, hbm, hbm, hbm, hbm], out_specs=vm,
        scratch_shapes=[
            pltpu.VMEM((512, KROWS), bf), pltpu.VMEM((128, 576), bf), pltpu.VMEM((8192 // T, KROWS, T), bf), pltpu.VMEM((512, T), f32), pltpu.VMEM((512, T), f32),
            pltpu.VMEM((512, 128), f32), pltpu.VMEM((512, 128), f32), pltpu.VMEM((512, 512), f32), pltpu.VMEM((64, 8, 512), bf),
            pltpu.VMEM((64, 8, 512), bf), pltpu.VMEM((512, 256), bf), pltpu.VMEM((256, COLS), bf), pltpu.VMEM((2, 2, COLS, 256), bf),
            pltpu.VMEM((512, COLS), bf), pltpu.VMEM((512, 256), bf), pltpu.VMEM((2, 512, 256), bf),
            pltpu.VMEM((4, 4, 4, 8, COLS), bf), pltpu.VMEM((4, 4, 4, 8, COLS), bf), pltpu.VMEM((3, 4, 8, COLS), bf), pltpu.VMEM((3, 8, COLS), bf),
            pltpu.VMEM((3, 8, COLS), f32), pltpu.VMEM((2, 4, 2 * COLS), bf), pltpu.VMEM((2, 4, 128), f32), pltpu.VMEM((4, 4, 4, 8, GCOLS), bf),
            pltpu.VMEM((2, 2, 512, 256), f32), pltpu.VMEM((2, 512, 256), bf), pltpu.VMEM((2, 512, 256), bf), pltpu.VMEM((512, 512), bf), pltpu.VMEM((3, 4, COLS), f32),
            dma((8192 // T,)), pltpu.SemaphoreType.REGULAR((2,)), dma, dma, dma((7,)), dma((7,)), dma((7,)), dma((5,)), dma((5,)),
            *[dma((GROUPS, 3, 12)) for _ in range(6)]],
        compiler_params=pltpu.CompilerParams(collective_id=1, has_side_effects=True, vmem_limit_bytes=60 << 20),
    )(lengths, qt, new, kt, ids, scores, residual, gain, uv, wo, wg, wu, wd)


def per_device(queries, new_latent, cache_latent, cache_len, route_ids, route_scores, residual, norm_gain,
               w_uv, w_out, w_gate, w_up, w_down):
    return layer_call(cache_len[None], jnp.swapaxes(queries[0], 1, 2), new_latent[0], jnp.swapaxes(cache_latent[0], 0, 1), route_ids[0], route_scores[0],
                      residual[0], norm_gain.reshape(56, 128), w_uv[0], w_out[0], w_gate[0], w_up[0], w_down[0])[None]


def solution(mesh):
    r = ("sec", "ep")
    placed = (P(r, None, None, None), P(r, None, None), P(r, None, None), P(r), P(r, None, None), P(r, None, None), P(r, None, None),
              P(), P(r, None, None), P(r, None, None), P("ep", None, "sec"), P("ep", None, "sec"), P("ep", "sec", None))
    return jax.shard_map(per_device, mesh=mesh, in_specs=placed, out_specs=P(r, None, None), check_vma=False)
```

```python
import functools
import jax, jax.numpy as jnp
from jax import lax
from jax.experimental import pallas as pl
from jax.experimental.pallas import tpu as pltpu
from jax.sharding import PartitionSpec as P

MESH = pl.DeviceIdType.MESH
f32 = jnp.float32
bf = jnp.bfloat16
COLS = 3584
GCOLS = 3712
ORDERS = ((0, 1, 2), (1, 2, 0), (2, 0, 1))


def streams(groups):
    start, made = 0, []
    for tiles, halves in groups:
        made.append([])
        for p in range(3):
            made[-1].append((start, tiles[p] * 128, halves[p] * 128, ORDERS[p]))
            start += tiles[p] * 128
    return made


RS = streams((((5, 5, 4), (3, 3, 2)), ((5, 4, 5), (2, 2, 2))))
AG = streams((((5, 5, 4), (3, 3, 2)), ((5, 5, 5), (2, 2, 3))))
GROUPS = len(RS)
WIDTH = COLS // GROUPS


def dev(pos, c):
    return (pos[0], (pos[1] * 4 + pos[2]) * 2 + c)


def shifted(pos, axis, by):
    out = list(pos)
    out[axis] = (pos[axis] + by) % 4
    return tuple(out)


def remote(src, dst, ss, rs, to):
    return pltpu.make_async_remote_copy(src_ref=src, dst_ref=dst, send_sem=ss, recv_sem=rs, device_id=to, device_id_type=MESH)


def region(pos, stream, stage, q, lo=0, hi=None):
    start, width, _, order = stream
    idx = [slice(None)] * 3
    for k in range(stage):
        idx[order[k]] = pos[order[k]]
    idx[order[stage]] = q
    return tuple(idx) + (slice(None), slice(start + lo, start + (width if hi is None else hi)))


def halves(stream):
    _, width, half, _ = stream
    return ((0, 1, 0, half), (1, 3, half, width))


def rests(stream):
    _, width, half, _ = stream
    return ((0, 1, half, width), (1, 3, 0, half))


class ReduceScatter:
    def __init__(self, pos, c, acc, bufs, ss, rs, out):
        self.pos, self.c, self.acc, self.bufs, self.ss, self.rs, self.out = pos, c, acc, bufs, ss, rs, out
        self.copies = {}

    def reg(self, st, stage, q, lo=0, hi=None):
        return self.acc.at[region(self.pos, st, stage, q, lo, hi)]

    def slot(self, st, stage, d, lo=0, hi=None):
        start, width = st[:2]
        return self.bufs[stage].at[(d,) + (slice(None),) * (2 - stage) + (slice(None), slice(start + lo, start + (width if hi is None else hi)))]

    def send(self, g, p, n, src, dst, axis, by):
        cp = remote(src, dst, self.ss.at[g, p, n], self.rs.at[g, p, n], dev(shifted(self.pos, axis, by), self.c))
        cp.start()
        self.copies[g, p, n] = cp

    def total(self, g, p, st, stage, first, count):
        axis = st[3][stage]
        total = self.reg(st, stage, self.pos[axis])[...].astype(f32)
        for d in range(count):
            self.copies[g, p, first + d].wait_recv()
            if stage == 0:
                self.copies[g, p, 10 + d].wait_recv()
            total += self.slot(st, stage, d)[...].astype(f32)
        return total

    def step(self, g, k):
        pos = self.pos
        for p, st in enumerate(RS[g]):
            start, width, _, order = st
            if k == 0:
                for d, by, lo, hi in halves(st):
                    self.send(g, p, d, self.reg(st, 0, (pos[order[0]] + 2) % 4, lo, hi), self.slot(st, 0, 2 + d, lo, hi), order[0], by)
            elif k == 1:
                for d, by, lo, hi in halves(st):
                    q = (pos[order[0]] + by) % 4
                    self.copies[g, p, d].wait_recv()
                    dst = self.reg(st, 0, q, lo, hi)
                    dst[...] = (dst[...].astype(f32) + self.slot(st, 0, 2 + d, lo, hi)[...].astype(f32)).astype(bf)
                    self.send(g, p, 2 + d, self.reg(st, 0, q, lo, hi), self.slot(st, 0, d, lo, hi), order[0], by)
            elif k in (2, 3):
                stage = k - 1
                mine = self.reg(st, stage - 1, pos[order[stage - 1]])
                mine[...] = (self.total(g, p, st, 0, 2, 2) if k == 2 else self.total(g, p, st, 1, 4, 3)).astype(bf)
                for by in (2, 1, 3):
                    q = (pos[order[stage]] + by) % 4
                    self.send(g, p, 1 + 3 * stage + by - 1, self.reg(st, stage, q), self.slot(st, stage, by - 1), order[stage], by)
            else:
                self.out[:, start:start + width] = self.total(g, p, st, 2, 7, 3)
        if k == 0:
            for p, st in enumerate(RS[g]):
                axis = st[3][0]
                for d, by, lo, hi in rests(st):
                    self.send(g, p, 10 + d, self.reg(st, 0, (pos[axis] + by) % 4, lo, hi), self.slot(st, 0, d, lo, hi), axis, by)

    def drain(self):
        for cp in self.copies.values():
            cp.wait_send()


class AllGather:
    def __init__(self, pos, c, g, ss, rs):
        self.pos, self.c, self.g, self.ss, self.rs = pos, c, g, ss, rs
        self.copies = {}

    def send(self, g, p, n, st, stage, q, lo, hi, axis, by):
        r = self.g.at[region(self.pos, st, stage, q, lo, hi)]
        cp = remote(r, r, self.ss.at[g, p, n], self.rs.at[g, p, n], dev(shifted(self.pos, axis, by), self.c))
        cp.start()
        self.copies[g, p, n] = cp

    def arrived(self, g, p, *which):
        for n in which:
            self.copies[g, p, n].wait_recv()

    def step(self, g, k):
        pos = self.pos
        for p, st in enumerate(AG[g]):
            order = st[3]
            if k in (0, 1):
                stage = 2 - k
                if k == 1:
                    self.arrived(g, p, 7, 8, 9)
                for by in (2, 1, 3):
                    self.send(g, p, 1 + 3 * stage + by - 1, st, stage, pos[order[stage]], 0, None, order[stage], by)
            elif k == 2:
                self.arrived(g, p, 4, 5, 6)
                for d, by, lo, hi in halves(st):
                    self.send(g, p, d, st, 0, pos[order[0]], lo, hi, order[0], by)
                for d, by, lo, hi in rests(st):
                    self.send(g, p, 10 + d, st, 0, pos[order[0]], lo, hi, order[0], by)
            elif k == 3:
                for d, by, lo, hi in halves(st):
                    self.arrived(g, p, d)
                    self.send(g, p, 2 + d, st, 0, (pos[order[0]] + 4 - by) % 4, lo, hi, order[0], by)
            else:
                self.arrived(g, p, 2, 3, 10, 11)

    def drain(self):
        for cp in self.copies.values():
            cp.wait_send()


T = 1024
KROWS = 592
SCORE = (192.0 ** -0.5) * 1.4426950408889634


def attention(len_ref, qt_ref, new_ref, kt_ref, q_sc, n_sc, kbuf, s_a, s_b, m_sc, l_sc, acc_sc, k_sem, between):
    blocks = kbuf.shape[0]
    copies = [pltpu.make_async_copy(kt_ref.at[:, i * T:(i + 1) * T], kbuf.at[i, 0:576, :], k_sem.at[i]) for i in range(blocks)]
    for cp in copies:
        cp.start()
    n = len_ref[0, 0]
    edge = lax.broadcasted_iota(jnp.int32, (16, T), 0)
    lane = lax.broadcasted_iota(jnp.int32, (16, T), 1)
    for i in range(blocks):
        kbuf[i, 576:592, :] = jnp.where((edge == 0) & (lane + i * T >= n), -1e30, 0.0).astype(bf)
    r0 = lax.broadcasted_iota(jnp.int32, (512, 512), 0)
    r1 = lax.broadcasted_iota(jnp.int32, (512, 512), 1)
    order = jnp.where((r0 % 4) * 128 + r0 // 4 == r1, 1.0, 0.0).astype(bf)
    q = jnp.concatenate([qt_ref[s].T for s in range(4)], axis=0)
    q_sc[:, 0:576] = jnp.dot(order, q, preferred_element_type=f32).astype(bf)
    q_sc[:, 576:592] = jnp.where(lax.broadcasted_iota(jnp.int32, (512, 16), 1) == 0, 1.0, 0.0).astype(bf)
    n_sc[...] = jnp.zeros_like(n_sc)
    n_sc[0:4, :] = new_ref[...]
    s = lax.dot_general(q_sc[:, 0:576], n_sc[...], (((1,), (1,)), ((), ())), preferred_element_type=f32) * SCORE
    row = lax.broadcasted_iota(jnp.int32, s.shape, 0)
    col = lax.broadcasted_iota(jnp.int32, s.shape, 1)
    s = jnp.where(col <= row % 4, s, -1e30)
    m = jnp.max(s, axis=1, keepdims=True)
    p = jnp.exp2(s - m)
    m_sc[...] = jnp.broadcast_to(m, (512, 128))
    l_sc[...] = jnp.broadcast_to(jnp.sum(p, axis=1, keepdims=True), (512, 128))
    acc_sc[...] = jnp.dot(p.astype(bf), n_sc[:, 0:512], preferred_element_type=f32)

    def scores(i, into):
        into[...] = jnp.dot(q_sc[...], kbuf[i], preferred_element_type=f32)

    def fold(i, s_ref):
        s = s_ref[...]
        old = m_sc[...]
        new = jnp.maximum(old, jnp.max(s, axis=1, keepdims=True) * SCORE)
        shrink = jnp.exp2(old - new)
        p = jnp.exp2(s * SCORE - new[:, 0:1])
        l_sc[...] = l_sc[...] * shrink + jnp.sum(p, axis=1, keepdims=True)
        m_sc[...] = new
        pv = lax.dot_general(p.astype(bf), kbuf[i, 0:512, :], (((1,), (1,)), ((), ())), preferred_element_type=f32)
        acc_sc[...] = acc_sc[...] * shrink[:, 0:1] + pv

    copies[0].wait()
    scores(0, s_a)
    for i in range(blocks):
        if i + 1 < blocks:
            copies[i + 1].wait()
            scores(i + 1, (s_a, s_b)[(i + 1) % 2])
        fold(i, (s_a, s_b)[i % 2])
        if i in between:
            between[i]()
    return acc_sc[...] * (1.0 / l_sc[:, 0:1])


def layer_kernel(len_ref, qt_ref, new_ref, kt_ref, ids_ref, sc_ref, res_ref, gain_ref, uv_hbm, wo_hbm, wg_hbm, wu_hbm, wd_hbm, out_ref,
                 q_sc, n_sc, kbuf, s_a, s_b, m_sc, l_sc, acc_sc, o_ref, x_v, uv_v, wo_v, w_v, wd_v, h_v, hs_v, acc, b0, b1, b2, part, res_v, cf_v, g_v, gu_v, snd_v, rcv_v, act_v, fin_v,
                 k_sem, t_sem, a_ss, a_rs, l_sem, w_ss, w_rs, s_ss, s_rs, r1_ss, r1_rs, g_ss, g_rs, r2_ss, r2_rs):
    z = lax.axis_index("sec")
    e = lax.axis_index("ep")
    x, y, c = e // 8, (e // 2) % 4, e % 2
    pos = (z, x, y)
    me = z * 16 + x * 4 + y
    sib = dev(pos, 1 - c)
    mine = pl.multiple_of(c * COLS, 128)
    other = pl.multiple_of((1 - c) * COLS, 128)

    def peer(i):
        k = (me + i) % 64
        return k, (k // 16, (k % 16) * 2 + c)

    barrier = pltpu.get_barrier_semaphore()

    def tell(axis, sem):
        for by in (1, 2, 3):
            pl.semaphore_signal(sem, inc=1, device_id=dev(shifted(pos, axis, by), c), device_id_type=MESH)

    for axis in range(3):
        tell(axis, barrier)
    pl.semaphore_signal(barrier, inc=1, device_id=sib, device_id_type=MESH)

    uvc = pl.ds(pl.multiple_of(c * 128, 128), 128)
    local = [pltpu.make_async_copy(a, b, l_sem.at[i]) for i, (a, b) in enumerate((
        (o_ref.at[me], x_v.at[me]),
        (uv_hbm, uv_v.at[:, uvc]),
        (wo_hbm.at[:, pl.ds(mine, COLS)], wo_v.at[pl.ds(pl.multiple_of(c * 128, 128), 128), :]),
        (wg_hbm.at[pl.ds(mine, COLS), :], w_v.at[c, 0]),
        (wu_hbm.at[pl.ds(mine, COLS), :], w_v.at[c, 1]),
        (wd_hbm.at[:, pl.ds(mine, COLS)], wd_v.at[pl.ds(pl.multiple_of(c * 256, 256), 256), :]),
        (res_ref, res_v.at[c]),
    ))]
    for i in (1, 2, 6):
        local[i].start()
    sc = sc_ref[...]
    shares = sc / jnp.sum(sc, axis=1, keepdims=True) * 2.5
    ids = ids_ref[...]
    lane = lax.broadcasted_iota(jnp.int32, (4, 128), 1)
    coef = jnp.zeros((4, 128), f32)
    for k in range(8):
        coef += jnp.where(lane % 32 == ids[:, k:k + 1], shares[:, k:k + 1], 0.0)
    high = coef.astype(bf).astype(f32)
    cf_v[c] = jnp.where(lane < 32, high, jnp.where(lane < 64, coef - high, 0.0))

    early = [remote(a, b, w_ss.at[i], w_rs.at[i], sib) for i, (a, b) in enumerate((
        (uv_hbm, uv_v.at[:, uvc]),
        (wo_hbm.at[:, pl.ds(other, COLS)], wo_v.at[pl.ds(pl.multiple_of(c * 128, 128), 128), :]),
        (wg_hbm.at[pl.ds(other, COLS), :], w_v.at[c, 0]),
        (wu_hbm.at[pl.ds(other, COLS), :], w_v.at[c, 1]),
        (wd_hbm.at[:, pl.ds(other, COLS)], wd_v.at[pl.ds(pl.multiple_of(c * 256, 256), 256), :]),
        (res_ref, res_v.at[c]),
        (cf_v.at[c], cf_v.at[c]),
    ))]
    def exchange_weights():
        pl.semaphore_wait(barrier, 10)
        tell(1, t_sem.at[0])
        for i in (0, 1, 5, 6, 2, 3, 4):
            early[i].start()
        for cp in local[3:6]:
            cp.start()

    def second_turn():
        pl.semaphore_wait(t_sem.at[0], 3)
        tell(2, t_sem.at[1])

    latent = attention(len_ref, qt_ref, new_ref, kt_ref, q_sc, n_sc, kbuf, s_a, s_b, m_sc, l_sc, acc_sc, k_sem, {1: exchange_weights, 4: second_turn})
    pl.semaphore_wait(t_sem.at[1], 3)
    o_ref.reshape(512, 512)[...] = latent.astype(bf)
    local[0].start()

    @pl.loop(1, 64, unroll=7)
    def _(i):
        k, to = peer(i)
        remote(o_ref.at[k], x_v.at[me], a_ss, a_rs, to).start()

    for i in (0, 1, 2):
        local[i].wait()
    for i in (0, 1):
        early[i].wait_recv()

    latents = remote(o_ref.at[pl.ds(0, 63)], x_v.at[pl.ds(0, 63)], a_ss, a_rs, sib)
    latents.wait_recv()

    m = jnp.dot(x_v.reshape(512, 512)[...], uv_v[...], preferred_element_type=f32)
    row = lax.broadcasted_iota(jnp.int32, (512, 256), 0)
    col = lax.broadcasted_iota(jnp.int32, (512, 256), 1)
    m = jnp.where((row // 4) % 2 == col // 128, m, 0.0).astype(bf)
    t = lax.broadcasted_iota(jnp.int32, (512, 512), 0)
    r = lax.broadcasted_iota(jnp.int32, (512, 512), 1)
    put = jnp.where((t // 8 == r // 8) & (t % 4 == r % 4) & ((t // 4) % 2 == c), 1.0, 0.0).astype(bf)
    hs_v[0] = jnp.dot(put, m, preferred_element_type=f32).astype(bf)
    swap = remote(hs_v.at[0], hs_v.at[1], s_ss.at[0], s_rs.at[0], sib)
    swap.start()
    swap.wait()
    h_v[...] = hs_v[0] + hs_v[1]
    acc2 = acc.reshape(512, COLS)

    def project(a, w, g):
        for half in range(2):
            cols = slice(g * WIDTH + half * (WIDTH // 2), g * WIDTH + (half + 1) * (WIDTH // 2))
            acc2[:, cols] = jnp.dot(a[...], w[:, cols], preferred_element_type=f32).astype(bf)

    def project_and_reduce(a, w, ss, rs, out, aside):
        sums = ReduceScatter(pos, c, acc, (b0, b1, b2), ss, rs, out)
        for k in range(5):
            for g in range(GROUPS):
                if k == 0:
                    project(a, w, g)
                sums.step(g, k)
            if k == 0:
                aside()
        return sums

    def sent_latents():
        latents.wait_send()
        for i in (0, 1):
            early[i].wait_send()

    sums = project_and_reduce(h_v, wo_v, r1_ss, r1_rs, part.at[0], sent_latents)
    swap = remote(part.at[0], part.at[1], s_ss.at[1], s_rs.at[1], sib)
    swap.start()
    sums.drain()
    local[6].wait()
    early[5].wait_recv()
    early[6].wait_recv()
    res8 = lambda cols: jnp.concatenate([res_v[0, :, cols].astype(f32), res_v[1, :, cols].astype(f32)], axis=0)
    swap.wait()
    part[0] += res8(pl.ds(mine, COLS))
    part[1] += res8(pl.ds(other, COLS))
    squares = jnp.sum(part[0] * part[0], axis=1, keepdims=True) + jnp.sum(part[1] * part[1], axis=1, keepdims=True)
    scale = lax.rsqrt(squares * (1.0 / (2 * COLS)) + 1e-06)
    gmine = g_v.at[z, x, y]
    gain = jnp.where(c == 0, gain_ref[0:28, :].astype(f32), gain_ref[28:56, :].astype(f32))
    gain = jnp.concatenate([gain[i:i + 1, :] for i in range(28)], axis=1)
    gmine[:, :COLS] = (part[0] * scale * gain).astype(bf)
    gmine[:, COLS:] = jnp.concatenate([cf_v[0], cf_v[1]], axis=0).astype(bf)

    gather = AllGather(pos, c, g_v, g_ss, g_rs)
    tokens = g_v.reshape(512, GCOLS)
    for k in range(4):
        for g in range(GROUPS):
            gather.step(g, k)
    for i in (3, 4):
        local[i].wait()
    for i in (2, 3):
        early[i].wait_recv()

    def product(which, gu, g):
        rows = slice(g * WIDTH, (g + 1) * WIDTH)
        return jnp.dot(tokens[:, rows], w_v[which, gu, rows, :], preferred_element_type=f32)

    for g in range(GROUPS):
        gather.step(g, 4)
        for n, which in ((0, 1 - c), (1, c)):
            for gu in (0, 1):
                new = product(which, gu, g)
                if g > 0:
                    new += gu_v[n, gu]
                if g < GROUPS - 1:
                    gu_v[n, gu] = new
                elif n == 0:
                    snd_v[gu] = new.astype(bf)
                else:
                    gu_v[n, gu] = new
            if n == 0 and g == GROUPS - 1:
                swap = remote(snd_v, rcv_v, s_ss.at[2], s_rs.at[2], sib)
                swap.start()
    coefs = tokens[:, COLS:].astype(f32)
    lane = lax.broadcasted_iota(jnp.int32, (512, 128), 1)
    column = jnp.sum(jnp.where((lane % 32 == e) & (lane < 64), coefs, 0.0), axis=1, keepdims=True)
    swap.wait()
    gate = gu_v[1, 0] + rcv_v[0].astype(f32)
    up = gu_v[1, 1] + rcv_v[1].astype(f32)
    acts = act_v.at[:, pl.ds(pl.multiple_of(c * 256, 256), 256)]
    acts[...] = (gate / (1.0 + jnp.exp(-gate)) * up * column).astype(bf)
    swap = remote(acts, acts, s_ss.at[3], s_rs.at[3], sib)
    swap.start()
    local[5].wait()
    early[4].wait_recv()
    swap.wait()
    def sent_tokens():
        for i in range(2, 7):
            early[i].wait_send()
        gather.drain()

    sums = project_and_reduce(act_v, wd_v, r2_ss, r2_rs, part.at[2], sent_tokens)
    fin_v[0] = part[2, 0:4, :]
    fin_v[1] = part[2, 4:8, :]
    swap = remote(fin_v.at[1 - c], fin_v.at[2], s_ss.at[4], s_rs.at[4], sib)
    swap.start()

    def own(v):
        return jnp.where(c == 0, v[0:4, :], v[4:8, :])
    out_ref[:, pl.ds(mine, COLS)] = (own(part[0]) + fin_v[c]).astype(bf)
    sums.drain()
    swap.wait()
    out_ref[:, pl.ds(other, COLS)] = (own(part[1]) + fin_v[2]).astype(bf)


def layer_call(lengths, qt, new, kt, ids, scores, residual, gain, uv, wo, wg, wu, wd):
    vm = pl.BlockSpec(memory_space=pltpu.VMEM)
    hbm = pl.BlockSpec(memory_space=pl.ANY)
    dma = pltpu.SemaphoreType.DMA
    return pl.pallas_call(
        layer_kernel, out_shape=jax.ShapeDtypeStruct((4, 2 * COLS), bf),
        in_specs=[pl.BlockSpec(memory_space=pltpu.SMEM), vm, vm, hbm, vm, vm, vm, vm, hbm, hbm, hbm, hbm, hbm], out_specs=vm,
        scratch_shapes=[
            pltpu.VMEM((512, KROWS), bf), pltpu.VMEM((128, 576), bf), pltpu.VMEM((8192 // T, KROWS, T), bf), pltpu.VMEM((512, T), f32), pltpu.VMEM((512, T), f32),
            pltpu.VMEM((512, 128), f32), pltpu.VMEM((512, 128), f32), pltpu.VMEM((512, 512), f32), pltpu.VMEM((64, 8, 512), bf),
            pltpu.VMEM((64, 8, 512), bf), pltpu.VMEM((512, 256), bf), pltpu.VMEM((256, COLS), bf), pltpu.VMEM((2, 2, COLS, 256), bf),
            pltpu.VMEM((512, COLS), bf), pltpu.VMEM((512, 256), bf), pltpu.VMEM((2, 512, 256), bf),
            pltpu.VMEM((4, 4, 4, 8, COLS), bf), pltpu.VMEM((4, 4, 4, 8, COLS), bf), pltpu.VMEM((3, 4, 8, COLS), bf), pltpu.VMEM((3, 8, COLS), bf),
            pltpu.VMEM((3, 8, COLS), f32), pltpu.VMEM((2, 4, 2 * COLS), bf), pltpu.VMEM((2, 4, 128), f32), pltpu.VMEM((4, 4, 4, 8, GCOLS), bf),
            pltpu.VMEM((2, 2, 512, 256), f32), pltpu.VMEM((2, 512, 256), bf), pltpu.VMEM((2, 512, 256), bf), pltpu.VMEM((512, 512), bf), pltpu.VMEM((3, 4, COLS), f32),
            dma((8192 // T,)), pltpu.SemaphoreType.REGULAR((2,)), dma, dma, dma((7,)), dma((7,)), dma((7,)), dma((5,)), dma((5,)),
            *[dma((GROUPS, 3, 12)) for _ in range(6)]],
        compiler_params=pltpu.CompilerParams(collective_id=1, has_side_effects=True, vmem_limit_bytes=60 << 20),
    )(lengths, qt, new, kt, ids, scores, residual, gain, uv, wo, wg, wu, wd)


def per_device(queries, new_latent, cache_latent, cache_len, route_ids, route_scores, residual, norm_gain,
               w_uv, w_out, w_gate, w_up, w_down):
    return layer_call(cache_len[None], jnp.swapaxes(queries[0], 1, 2), new_latent[0], jnp.swapaxes(cache_latent[0], 0, 1), route_ids[0], route_scores[0],
                      residual[0], norm_gain.reshape(56, 128), w_uv[0], w_out[0], w_gate[0], w_up[0], w_down[0])[None]


def solution(mesh):
    r = ("sec", "ep")
    placed = (P(r, None, None, None), P(r, None, None), P(r, None, None), P(r), P(r, None, None), P(r, None, None), P(r, None, None),
              P(), P(r, None, None), P(r, None, None), P("ep", None, "sec"), P("ep", None, "sec"), P("ep", "sec", None))
    return jax.shard_map(per_device, mesh=mesh, in_specs=placed, out_specs=P(r, None, None), check_vma=False)
```
